32 devices in a mesh: ep: 8 (over z, y), dp: 4 (over x, core).
Axes of the slice: x: 2, y: 2, z: 4, core: 2. Of those that a mesh axis runs over, the one named last changes fastest.
Arguments:
- tokens: bfloat16 [1024, 2048], P(('ep', 'dp')), may hold values from -6 to 6
- cotangent: bfloat16 [1024, 2048], P(('ep', 'dp')), may hold values from -6 to 6
- expert_ids: int32 [1024, 8], P(('ep', 'dp')), may hold values from 0 to 7, as said below
- route_weights: bfloat16 [1024, 8], P(('ep', 'dp')), may hold values from 0.049804688 to 0.5
- w_gate: bfloat16 [8, 2048, 768], P('ep'), may hold values from -0.125 to 0.125
- w_up: bfloat16 [8, 2048, 768], P('ep'), may hold values from -0.125 to 0.125
- w_down: bfloat16 [8, 768, 2048], P('ep'), may hold values from -0.21875 to 0.21875
Outputs:
- grad_tokens: bfloat16 [1024, 2048], P(('ep', 'dp'))
- grad_route: bfloat16 [1024, 8], P(('ep', 'dp'))
- grad_gate: bfloat16 [8, 2048, 768], P('ep', 'dp')
- grad_up: bfloat16 [8, 2048, 768], P('ep', 'dp')
- grad_down: bfloat16 [8, 768, 2048], P('ep', None, 'dp')
The draws below stay inside these ranges and needn't reach their ends.
Inputs may be any that keep to these rules, and one draw needn't show every extreme that they name: `expert_ids`: each token names 8 different experts. The tokens of one device name no expert more than 32 times; 1 expert, drawn from the seed, are named exactly 32 times by every device's tokens.
All inputs are finite; a program needn't handle non-finite values.
Results may differ from the reference program's by a relative error of at most 0.0095.
Values may be sent and summed in bfloat16 or wider, within the bound.
A program may use at most 128 MiB of HBM per device.

```python
import math
import jax
import jax.numpy as jnp
from jax import lax

D = 2048
FF = 768
TOPK = 8
TOK_DEV = 32
EXPERTS = 8
CAP = 32
HOT = 1
TOKENS = 1024
N_EP = 8
N_DP = 4


def draw_expert_ids(key, part):
    blocks = TOKENS // TOK_DEV
    half_count = EXPERTS // 2
    hot_key = jax.random.fold_in(key, 11)
    pair_pick = jax.random.permutation(jax.random.fold_in(hot_key, 1), half_count)[:HOT].astype(jnp.int32)
    side_pick = jax.random.randint(jax.random.fold_in(hot_key, 2), (HOT,), 0, 2).astype(jnp.int32)
    hot_ids = pair_pick + side_pick * half_count
    is_hot = jnp.zeros((EXPERTS,), jnp.int32).at[hot_ids].set(1)
    tickets = EXPERTS * CAP
    ticket_owner = jnp.arange(tickets, dtype=jnp.int32) // CAP
    row_total = TOK_DEV * TOPK

    def one_block(index):
        block_key = jax.random.fold_in(jax.random.fold_in(key, 23), index)
        ranking = jax.random.permutation(jax.random.fold_in(block_key, 1), tickets).astype(jnp.int32)
        score = (1 - is_hot[ticket_owner]) * tickets + ranking
        chosen = jnp.argsort(score, stable=True)[:row_total]
        listed = jnp.sort(ticket_owner[chosen])
        slot_pos = jnp.arange(row_total, dtype=jnp.int32)
        token_pos = slot_pos % TOK_DEV
        column_pos = slot_pos // TOK_DEV
        shuffle = jax.random.permutation(jax.random.fold_in(block_key, 2), TOK_DEV).astype(jnp.int32)
        turned = jax.random.randint(jax.random.fold_in(block_key, 3), (TOK_DEV,), 0, TOPK).astype(jnp.int32)
        new_token = shuffle[token_pos]
        new_column = (column_pos + turned[new_token]) % TOPK
        return jnp.zeros((TOK_DEV, TOPK), jnp.int32).at[new_token, new_column].set(listed)
    drawn = lax.map(one_block, jnp.arange(blocks, dtype=jnp.int32))
    return drawn.reshape(TOKENS, TOPK)


def steps_of(rng, extent, split, low, high):
    level, own = 1.0, jax.random.fold_in(rng, 6)
    for position, blocks in split:
        draws = jnp.exp(jax.random.uniform(jax.random.fold_in(own, position), (blocks,), jnp.float32, low / len(split), high / len(split)))
        level = level * jnp.repeat(draws, extent[position] // blocks).reshape([-1 if axis == position else 1 for axis in range(len(extent))])
    return level


def centred(own_key, dims, scale, reach, shards=(), kind=jnp.bfloat16):
    array = scale * jax.random.normal(own_key, dims, jnp.float32)
    if shards:
        array = array * steps_of(own_key, dims, shards, -0.22, 0.18)
    return jnp.clip(array, -reach, reach).astype(kind)


def setup_inputs(seed: int = 0) -> dict:
    streams_of = jax.random.split(jax.random.key(seed), 8)
    tokens = centred(streams_of[0], (TOKENS, D), 1.0, 6.0, ((0, 32),))
    cotangent = centred(streams_of[1], (TOKENS, D), 1.0, 6.0, ((0, 32),))
    expert_ids = draw_expert_ids(jax.random.fold_in(streams_of[7], 71), 0)
    route_weights = jnp.clip(jnp.exp(math.log(0.5) - 2.306499 * jax.random.uniform(streams_of[3], (TOKENS, TOPK), jnp.float32) ** steps_of(streams_of[3], (TOKENS, TOPK), ((0, 32),), -0.2, 0.2)), 0.049804688, 0.5).astype(jnp.bfloat16)
    w_gate = centred(streams_of[4], (EXPERTS, D, FF), D ** -0.5, 0.125, ((0, 8),))
    w_up = centred(streams_of[5], (EXPERTS, D, FF), D ** -0.5, 0.125, ((0, 8),))
    w_down = centred(streams_of[6], (EXPERTS, FF, D), FF ** -0.5, 0.21875, ((0, 8),))
    return {"tokens": tokens, "cotangent": cotangent, "expert_ids": expert_ids, "route_weights": route_weights, "w_gate": w_gate, "w_up": w_up, "w_down": w_down}


contract_last = (((1,), (1,)), ((), ()))
contract_first = (((0,), (0,)), ((), ()))


def silu_parts(gate_pre):
    sig = jax.nn.sigmoid(gate_pre)
    return gate_pre * sig, sig * (1.0 + gate_pre * (1.0 - sig))


def expert_rows(tok_rows, cot_rows, weight, w_gate_one, w_up_one, w_down_one):
    gate_pre = jnp.dot(tok_rows, w_gate_one, preferred_element_type=jnp.float32)
    up_pre = jnp.dot(tok_rows, w_up_one, preferred_element_type=jnp.float32)
    act, slope = silu_parts(gate_pre)
    hidden = lax.optimization_barrier((act * up_pre).astype(jnp.bfloat16))
    back = lax.dot_general(cot_rows, w_down_one, contract_last, preferred_element_type=jnp.float32)
    route_grad = jnp.sum(hidden.astype(jnp.float32) * back, axis=1)
    scaled = weight * back
    grad_gate_pre = (scaled * up_pre * slope).astype(jnp.bfloat16)
    grad_up_pre = (scaled * act).astype(jnp.bfloat16)
    scaled_cot = (weight * cot_rows.astype(jnp.float32)).astype(jnp.bfloat16)
    slot_grad = lax.dot_general(grad_gate_pre, w_gate_one, contract_last, preferred_element_type=jnp.float32)
    slot_grad = slot_grad + lax.dot_general(grad_up_pre, w_up_one, contract_last, preferred_element_type=jnp.float32)
    part_gate = lax.dot_general(tok_rows, grad_gate_pre, contract_first, preferred_element_type=jnp.float32)
    part_up = lax.dot_general(tok_rows, grad_up_pre, contract_first, preferred_element_type=jnp.float32)
    part_down = lax.dot_general(hidden, scaled_cot, contract_first, preferred_element_type=jnp.float32)
    return slot_grad, route_grad, part_gate, part_up, part_down


def reference(tokens, cotangent, expert_ids, route_weights, w_gate, w_up, w_down):
    slots = TOKENS * TOPK
    rows = N_EP * CAP
    flat_ids = expert_ids.reshape(slots)
    flat_w = route_weights.reshape(slots)
    slot_index = jnp.arange(slots, dtype=jnp.int32)
    group_of = (slot_index // (TOK_DEV * TOPK)) % N_DP

    def one_expert(expert):
        w_gate_one = w_gate[expert]
        w_up_one = w_up[expert]
        w_down_one = w_down[expert]
        total_gate = jnp.zeros((D, FF), jnp.float32)
        total_up = jnp.zeros((D, FF), jnp.float32)
        total_down = jnp.zeros((FF, D), jnp.float32)
        slot_list = []
        route_list = []
        target_list = []
        for group in range(N_DP):
            keyed = jnp.where((flat_ids == expert) & (group_of == group), slot_index, slots)
            order = jnp.argsort(keyed, stable=True)[:rows].astype(jnp.int32)
            valid = keyed[order] < slots
            pick = jnp.where(valid, order, 0).astype(jnp.int32)
            mask = valid.astype(tokens.dtype)[:, None]
            tok_rows = tokens[pick // TOPK] * mask
            cot_rows = cotangent[pick // TOPK] * mask
            weight = (flat_w[pick] * valid.astype(flat_w.dtype)).astype(jnp.float32)[:, None]
            result = expert_rows(tok_rows, cot_rows, weight, w_gate_one, w_up_one, w_down_one)
            slot_list.append(result[0].astype(jnp.bfloat16))
            route_list.append(result[1].astype(jnp.bfloat16))
            target_list.append(jnp.where(valid, order, slots).astype(jnp.int32))
            total_gate = total_gate + lax.optimization_barrier(result[2].astype(jnp.bfloat16)).astype(jnp.float32)
            total_up = total_up + lax.optimization_barrier(result[3].astype(jnp.bfloat16)).astype(jnp.float32)
            total_down = total_down + lax.optimization_barrier(result[4].astype(jnp.bfloat16)).astype(jnp.float32)
        return (jnp.stack(slot_list), jnp.stack(route_list), jnp.stack(target_list),
                total_gate.astype(jnp.bfloat16), total_up.astype(jnp.bfloat16), total_down.astype(jnp.bfloat16))

    outs = lax.map(one_expert, jnp.arange(EXPERTS, dtype=jnp.int32))
    targets = outs[2].reshape(-1)
    placed = jnp.zeros((slots + 1, D), jnp.float32).at[targets].set(outs[0].reshape(-1, D).astype(jnp.float32))[:slots]
    grad_tokens = jnp.sum(placed.reshape(TOKENS, TOPK, D), axis=1).astype(jnp.bfloat16)
    grad_route = jnp.zeros((slots + 1,), jnp.bfloat16).at[targets].set(outs[1].reshape(-1))[:slots].reshape(TOKENS, TOPK)
    return grad_tokens, grad_route, outs[3], outs[4], outs[5]
```

```python
import jax
import jax.numpy as jnp
from jax import lax
from jax.sharding import PartitionSpec as P

block_rows = 128
contract_last = (((1,), (1,)), ((), ()))
contract_first = (((0,), (0,)), ((), ()))


def silu_parts(gate_pre):
    sig = jax.nn.sigmoid(gate_pre)
    return (gate_pre * sig, sig * (1.0 + gate_pre * (1.0 - sig)))


def expert_pass(rows_x, rows_cot, rows_w, live_count, w_gate_one, w_up_one, w_down_one):
    total, model = rows_x.shape
    width = w_gate_one.shape[1]

    def step(index, carry):
        acc_gate, acc_up, acc_down, slot_grad, route_grad = carry
        start = index * block_rows
        tok = lax.dynamic_slice_in_dim(rows_x, start, block_rows, 0)
        cot = lax.dynamic_slice_in_dim(rows_cot, start, block_rows, 0)
        weight = lax.dynamic_slice_in_dim(rows_w, start, block_rows, 0).astype(jnp.float32)[:, None]
        gate_pre = jnp.dot(tok, w_gate_one, preferred_element_type=jnp.float32)
        up_pre = jnp.dot(tok, w_up_one, preferred_element_type=jnp.float32)
        act, slope = silu_parts(gate_pre)
        hidden = lax.optimization_barrier((act * up_pre).astype(jnp.bfloat16))
        back = lax.dot_general(cot, w_down_one, contract_last, preferred_element_type=jnp.float32)
        route_part = jnp.sum(hidden.astype(jnp.float32) * back, axis=1)
        scaled = weight * back
        grad_gate_pre = (scaled * up_pre * slope).astype(jnp.bfloat16)
        grad_up_pre = (scaled * act).astype(jnp.bfloat16)
        scaled_cot = (weight * cot.astype(jnp.float32)).astype(jnp.bfloat16)
        part = lax.dot_general(
            grad_gate_pre, w_gate_one, contract_last, preferred_element_type=jnp.float32
        )
        part = part + lax.dot_general(
            grad_up_pre, w_up_one, contract_last, preferred_element_type=jnp.float32
        )
        acc_gate = acc_gate + lax.dot_general(
            tok, grad_gate_pre, contract_first, preferred_element_type=jnp.float32
        )
        acc_up = acc_up + lax.dot_general(
            tok, grad_up_pre, contract_first, preferred_element_type=jnp.float32
        )
        acc_down = acc_down + lax.dot_general(
            hidden, scaled_cot, contract_first, preferred_element_type=jnp.float32
        )
        slot_grad = lax.dynamic_update_slice_in_dim(slot_grad, part, start, 0)
        route_grad = lax.dynamic_update_slice_in_dim(route_grad, route_part, start, 0)
        return (acc_gate, acc_up, acc_down, slot_grad, route_grad)

    init = (
        jnp.zeros((model, width), jnp.float32),
        jnp.zeros((model, width), jnp.float32),
        jnp.zeros((width, model), jnp.float32),
        jnp.zeros((total, model), jnp.float32),
        jnp.zeros((total,), jnp.float32),
    )
    block_count = (live_count + block_rows - 1) // block_rows
    return lax.fori_loop(0, block_count, step, init)


def routed_body(tokens, cotangent, expert_ids, route_weights, w_gate, w_up, w_down):
    tok_count, topk = expert_ids.shape
    model = tokens.shape[1]
    experts = lax.axis_size("ep")
    capacity = min(tok_count, 2 * tok_count * topk // experts)
    slots = tok_count * topk
    row_total = experts * capacity
    flat_ids = expert_ids.reshape(slots)
    onehot = (flat_ids[:, None] == jnp.arange(experts, dtype=jnp.int32)[None, :]).astype(jnp.int32)
    position = jnp.sum((jnp.cumsum(onehot, axis=0) - 1) * onehot, axis=1)
    slot_ids = jnp.arange(slots, dtype=jnp.int32)
    source = (
        jnp.full((row_total,), slots, jnp.int32).at[flat_ids * capacity + position].set(slot_ids)
    )
    filled = source < slots
    source_token = jnp.where(filled, source // topk, tok_count)
    joined = jnp.concatenate([tokens, cotangent], axis=1)
    picked = jnp.take(joined, source_token, axis=0, mode="fill", fill_value=0)
    send_x = picked[:, :model].reshape(experts, capacity, model)
    send_cot = picked[:, model:].reshape(experts, capacity, model)
    send_w = jnp.take(
        route_weights.reshape(slots), jnp.where(filled, source, slots), mode="fill", fill_value=0
    ).reshape(experts, capacity)
    recv_x, recv_cot, recv_w = (
        lax.all_to_all(send_x, "ep", split_axis=0, concat_axis=0, tiled=True),
        lax.all_to_all(send_cot, "ep", split_axis=0, concat_axis=0, tiled=True),
        lax.all_to_all(send_w, "ep", split_axis=0, concat_axis=0, tiled=True),
    )
    flat_w = recv_w.reshape(row_total)
    live = (flat_w != 0).astype(jnp.int32)
    live_count = jnp.sum(live)
    place = jnp.where(live > 0, jnp.cumsum(live) - 1, row_total)
    anchor = (
        jnp.full((row_total,), row_total, jnp.int32)
        .at[place]
        .set(jnp.arange(row_total, dtype=jnp.int32), mode="drop")
    )
    recv_joined = jnp.concatenate(
        [recv_x.reshape(row_total, model), recv_cot.reshape(row_total, model)], axis=1
    )
    packed = jnp.take(recv_joined, anchor, axis=0, mode="fill", fill_value=0)
    pack_x = packed[:, :model]
    pack_cot = packed[:, model:]
    pack_w = jnp.take(flat_w, anchor, mode="fill", fill_value=0)
    w_gate_one = w_gate[0]
    w_up_one = w_up[0]
    w_down_one = w_down[0]
    acc_gate, acc_up, acc_down, slot_grad, route_grad = expert_pass(
        pack_x, pack_cot, pack_w, live_count, w_gate_one, w_up_one, w_down_one
    )
    slot_rows = jnp.take(slot_grad, place, axis=0, mode="fill", fill_value=0.0).astype(jnp.bfloat16)
    route_rows = jnp.take(route_grad, place, axis=0, mode="fill", fill_value=0.0).astype(
        jnp.bfloat16
    )
    back_x, back_route_rows = (
        lax.all_to_all(
            slot_rows.reshape(experts, capacity, model),
            "ep",
            split_axis=0,
            concat_axis=0,
            tiled=True,
        ),
        lax.all_to_all(
            route_rows.reshape(experts, capacity), "ep", split_axis=0, concat_axis=0, tiled=True
        ),
    )
    mine_rows = back_x[flat_ids, position].reshape(tok_count, topk, model)
    grad_tokens = jnp.sum(mine_rows.astype(jnp.float32), axis=1).astype(jnp.bfloat16)
    grad_route = back_route_rows[flat_ids, position].reshape(tok_count, topk)
    summed = (
        lax.psum_scatter(
            acc_gate[None].astype(jnp.bfloat16), "dp", scatter_dimension=1, tiled=True
        ).astype(jnp.float32),
        lax.psum_scatter(
            acc_up[None].astype(jnp.bfloat16), "dp", scatter_dimension=1, tiled=True
        ).astype(jnp.float32),
        lax.psum_scatter(
            acc_down[None].astype(jnp.bfloat16), "dp", scatter_dimension=2, tiled=True
        ).astype(jnp.float32),
    )
    return (
        grad_tokens,
        grad_route,
        summed[0].astype(jnp.bfloat16),
        summed[1].astype(jnp.bfloat16),
        summed[2].astype(jnp.bfloat16),
    )


def dense_weights(expert_ids, route_weights, experts):
    named = expert_ids[:, :, None] == jnp.arange(experts, dtype=jnp.int32)[None, None, :]
    weights = route_weights.astype(jnp.float32)[:, :, None]
    return jnp.sum(jnp.where(named, weights, 0.0), axis=1)


def pick_route(table, expert_ids):
    experts = table.shape[0]
    named = expert_ids[:, :, None] == jnp.arange(experts, dtype=jnp.int32)[None, None, :]
    spread = table.astype(jnp.float32).T[:, None, :]
    return jnp.sum(jnp.where(named, spread, 0.0), axis=2).astype(jnp.bfloat16)


def dense_body(tokens, cotangent, expert_ids, route_weights, w_gate, w_up, w_down):
    tok_count, topk = expert_ids.shape
    model = tokens.shape[1]
    experts = lax.axis_size("ep")
    groups = lax.axis_size("dp")
    width = w_gate.shape[2]
    rows = experts * tok_count
    w_gate_one = w_gate[0]
    w_up_one = w_up[0]
    w_down_one = w_down[0]
    weights = dense_weights(expert_ids, route_weights, experts).astype(jnp.bfloat16)
    weight = lax.all_to_all(weights.T, "ep", split_axis=0, concat_axis=0, tiled=True)
    weight = weight.reshape(rows, 1).astype(jnp.float32)
    tok = lax.all_gather(tokens, "ep", axis=0, tiled=True)
    cot = lax.all_gather(cotangent, "ep", axis=0, tiled=True)
    gate_pre = jnp.dot(tok, w_gate_one, preferred_element_type=jnp.float32)
    up_pre = jnp.dot(tok, w_up_one, preferred_element_type=jnp.float32)
    act, slope = silu_parts(gate_pre)
    hidden = (act * up_pre).astype(jnp.bfloat16)
    back = lax.dot_general(cot, w_down_one, contract_last, preferred_element_type=jnp.float32)
    route_part = jnp.sum(hidden.astype(jnp.float32) * back, axis=1)
    scaled = weight * back
    grad_gate_pre = (scaled * up_pre * slope).astype(jnp.bfloat16)
    grad_up_pre = (scaled * act).astype(jnp.bfloat16)
    scaled_cot = (weight * cot.astype(jnp.float32)).astype(jnp.bfloat16)
    part = lax.dot_general(
        grad_gate_pre, w_gate_one, contract_last, preferred_element_type=jnp.float32
    )
    part = part + lax.dot_general(
        grad_up_pre, w_up_one, contract_last, preferred_element_type=jnp.float32
    )
    grad_tokens = lax.psum_scatter(
        part.astype(jnp.bfloat16), "ep", scatter_dimension=0, tiled=True
    )
    route_table = lax.all_to_all(
        route_part.astype(jnp.bfloat16).reshape(experts, tok_count),
        "ep",
        split_axis=0,
        concat_axis=0,
        tiled=True,
    )
    grad_route = pick_route(route_table, expert_ids)
    tok_cols = lax.all_to_all(tok, "dp", split_axis=1, concat_axis=0, tiled=True)
    cot_cols = lax.all_to_all(scaled_cot, "dp", split_axis=1, concat_axis=0, tiled=True)
    hidden_all = lax.all_gather(hidden, "dp", axis=0, tiled=True)
    gate_all = lax.all_gather(grad_gate_pre, "dp", axis=0, tiled=True)
    up_all = lax.all_gather(grad_up_pre, "dp", axis=0, tiled=True)
    grad_gate = lax.dot_general(tok_cols, gate_all, contract_first, preferred_element_type=jnp.float32)
    grad_up = lax.dot_general(tok_cols, up_all, contract_first, preferred_element_type=jnp.float32)
    grad_down = lax.dot_general(
        hidden_all, cot_cols, contract_first, preferred_element_type=jnp.float32
    )
    return (
        grad_tokens,
        grad_route,
        grad_gate[None].astype(jnp.bfloat16),
        grad_up[None].astype(jnp.bfloat16),
        grad_down[None].astype(jnp.bfloat16),
    )


def body(tokens, cotangent, expert_ids, route_weights, w_gate, w_up, w_down):
    tok_count, topk = expert_ids.shape
    experts = lax.axis_size("ep")
    whole = 2 * tok_count * topk // experts >= tok_count
    chosen = dense_body if whole else routed_body
    return chosen(tokens, cotangent, expert_ids, route_weights, w_gate, w_up, w_down)


def solution(mesh):
    return jax.shard_map(
        body,
        mesh=mesh,
        in_specs=(
            P(("ep", "dp"), None),
            P(("ep", "dp"), None),
            P(("ep", "dp"), None),
            P(("ep", "dp"), None),
            P("ep", None, None),
            P("ep", None, None),
            P("ep", None, None),
        ),
        out_specs=(
            P(("ep", "dp"), None),
            P(("ep", "dp"), None),
            P("ep", "dp", None),
            P("ep", "dp", None),
            P("ep", None, "dp"),
        ),
        check_vma=False,
    )
```

```python
import jax
import jax.numpy as jnp
from jax import lax
from jax.experimental import pallas as pl
from jax.experimental.pallas import tpu as pltpu
from jax.sharding import PartitionSpec as P

block_rows = 128
contract_last = (((1,), (1,)), ((), ()))
contract_first = (((0,), (0,)), ((), ()))


def silu_parts(gate_pre):
    sig = jax.nn.sigmoid(gate_pre)
    return (gate_pre * sig, sig * (1.0 + gate_pre * (1.0 - sig)))


def expert_pass(rows_x, rows_cot, rows_w, live_count, w_gate_one, w_up_one, w_down_one):
    total, model = rows_x.shape
    width = w_gate_one.shape[1]

    def step(index, carry):
        acc_gate, acc_up, acc_down, slot_grad, route_grad = carry
        start = index * block_rows
        tok = lax.dynamic_slice_in_dim(rows_x, start, block_rows, 0)
        cot = lax.dynamic_slice_in_dim(rows_cot, start, block_rows, 0)
        weight = lax.dynamic_slice_in_dim(rows_w, start, block_rows, 0).astype(jnp.float32)[:, None]
        gate_pre = jnp.dot(tok, w_gate_one, preferred_element_type=jnp.float32)
        up_pre = jnp.dot(tok, w_up_one, preferred_element_type=jnp.float32)
        act, slope = silu_parts(gate_pre)
        hidden = lax.optimization_barrier((act * up_pre).astype(jnp.bfloat16))
        back = lax.dot_general(cot, w_down_one, contract_last, preferred_element_type=jnp.float32)
        route_part = jnp.sum(hidden.astype(jnp.float32) * back, axis=1)
        scaled = weight * back
        grad_gate_pre = (scaled * up_pre * slope).astype(jnp.bfloat16)
        grad_up_pre = (scaled * act).astype(jnp.bfloat16)
        scaled_cot = (weight * cot.astype(jnp.float32)).astype(jnp.bfloat16)
        part = lax.dot_general(
            grad_gate_pre, w_gate_one, contract_last, preferred_element_type=jnp.float32
        )
        part = part + lax.dot_general(
            grad_up_pre, w_up_one, contract_last, preferred_element_type=jnp.float32
        )
        acc_gate = acc_gate + lax.dot_general(
            tok, grad_gate_pre, contract_first, preferred_element_type=jnp.float32
        )
        acc_up = acc_up + lax.dot_general(
            tok, grad_up_pre, contract_first, preferred_element_type=jnp.float32
        )
        acc_down = acc_down + lax.dot_general(
            hidden, scaled_cot, contract_first, preferred_element_type=jnp.float32
        )
        slot_grad = lax.dynamic_update_slice_in_dim(slot_grad, part, start, 0)
        route_grad = lax.dynamic_update_slice_in_dim(route_grad, route_part, start, 0)
        return (acc_gate, acc_up, acc_down, slot_grad, route_grad)

    init = (
        jnp.zeros((model, width), jnp.float32),
        jnp.zeros((model, width), jnp.float32),
        jnp.zeros((width, model), jnp.float32),
        jnp.zeros((total, model), jnp.float32),
        jnp.zeros((total,), jnp.float32),
    )
    block_count = (live_count + block_rows - 1) // block_rows
    return lax.fori_loop(0, block_count, step, init)


def routed_body(tokens, cotangent, expert_ids, route_weights, w_gate, w_up, w_down):
    tok_count, topk = expert_ids.shape
    model = tokens.shape[1]
    experts = lax.axis_size("ep")
    capacity = min(tok_count, 2 * tok_count * topk // experts)
    slots = tok_count * topk
    row_total = experts * capacity
    flat_ids = expert_ids.reshape(slots)
    onehot = (flat_ids[:, None] == jnp.arange(experts, dtype=jnp.int32)[None, :]).astype(jnp.int32)
    position = jnp.sum((jnp.cumsum(onehot, axis=0) - 1) * onehot, axis=1)
    slot_ids = jnp.arange(slots, dtype=jnp.int32)
    source = (
        jnp.full((row_total,), slots, jnp.int32).at[flat_ids * capacity + position].set(slot_ids)
    )
    filled = source < slots
    source_token = jnp.where(filled, source // topk, tok_count)
    joined = jnp.concatenate([tokens, cotangent], axis=1)
    picked = jnp.take(joined, source_token, axis=0, mode="fill", fill_value=0)
    send_x = picked[:, :model].reshape(experts, capacity, model)
    send_cot = picked[:, model:].reshape(experts, capacity, model)
    send_w = jnp.take(
        route_weights.reshape(slots), jnp.where(filled, source, slots), mode="fill", fill_value=0
    ).reshape(experts, capacity)
    recv_x, recv_cot, recv_w = (
        lax.all_to_all(send_x, "ep", split_axis=0, concat_axis=0, tiled=True),
        lax.all_to_all(send_cot, "ep", split_axis=0, concat_axis=0, tiled=True),
        lax.all_to_all(send_w, "ep", split_axis=0, concat_axis=0, tiled=True),
    )
    flat_w = recv_w.reshape(row_total)
    live = (flat_w != 0).astype(jnp.int32)
    live_count = jnp.sum(live)
    place = jnp.where(live > 0, jnp.cumsum(live) - 1, row_total)
    anchor = (
        jnp.full((row_total,), row_total, jnp.int32)
        .at[place]
        .set(jnp.arange(row_total, dtype=jnp.int32), mode="drop")
    )
    recv_joined = jnp.concatenate(
        [recv_x.reshape(row_total, model), recv_cot.reshape(row_total, model)], axis=1
    )
    packed = jnp.take(recv_joined, anchor, axis=0, mode="fill", fill_value=0)
    pack_x = packed[:, :model]
    pack_cot = packed[:, model:]
    pack_w = jnp.take(flat_w, anchor, mode="fill", fill_value=0)
    w_gate_one = w_gate[0]
    w_up_one = w_up[0]
    w_down_one = w_down[0]
    acc_gate, acc_up, acc_down, slot_grad, route_grad = expert_pass(
        pack_x, pack_cot, pack_w, live_count, w_gate_one, w_up_one, w_down_one
    )
    slot_rows = jnp.take(slot_grad, place, axis=0, mode="fill", fill_value=0.0).astype(jnp.bfloat16)
    route_rows = jnp.take(route_grad, place, axis=0, mode="fill", fill_value=0.0).astype(
        jnp.bfloat16
    )
    back_x, back_route_rows = (
        lax.all_to_all(
            slot_rows.reshape(experts, capacity, model),
            "ep",
            split_axis=0,
            concat_axis=0,
            tiled=True,
        ),
        lax.all_to_all(
            route_rows.reshape(experts, capacity), "ep", split_axis=0, concat_axis=0, tiled=True
        ),
    )
    mine_rows = back_x[flat_ids, position].reshape(tok_count, topk, model)
    grad_tokens = jnp.sum(mine_rows.astype(jnp.float32), axis=1).astype(jnp.bfloat16)
    grad_route = back_route_rows[flat_ids, position].reshape(tok_count, topk)
    summed = (
        lax.psum_scatter(
            acc_gate[None].astype(jnp.bfloat16), "dp", scatter_dimension=1, tiled=True
        ).astype(jnp.float32),
        lax.psum_scatter(
            acc_up[None].astype(jnp.bfloat16), "dp", scatter_dimension=1, tiled=True
        ).astype(jnp.float32),
        lax.psum_scatter(
            acc_down[None].astype(jnp.bfloat16), "dp", scatter_dimension=2, tiled=True
        ).astype(jnp.float32),
    )
    return (
        grad_tokens,
        grad_route,
        summed[0].astype(jnp.bfloat16),
        summed[1].astype(jnp.bfloat16),
        summed[2].astype(jnp.bfloat16),
    )


def dense_weights(expert_ids, route_weights, experts):
    named = expert_ids[:, :, None] == jnp.arange(experts, dtype=jnp.int32)[None, None, :]
    weights = route_weights.astype(jnp.float32)[:, :, None]
    return jnp.sum(jnp.where(named, weights, 0.0), axis=1)


def pick_route(table, expert_ids):
    experts = table.shape[0]
    named = expert_ids[:, :, None] == jnp.arange(experts, dtype=jnp.int32)[None, None, :]
    spread = table.astype(jnp.float32).T[:, None, :]
    return jnp.sum(jnp.where(named, spread, 0.0), axis=2).astype(jnp.bfloat16)


def fused_kernel(
    tok_hbm, cot_hbm, wd_ref, wg_hbm, wu_hbm, wdn_hbm,
    gt_ref, route_ref, gg_ref, gu_ref, gd_ref,
    wg, wu, wdn, tc, wbuf, cols, colst, h_own, h_recv, part, ys, yr, zs, zr, rs, rr,
    l_sem, w_send, w_recv, g_send, g_recv, c_send, c_recv,
    h_send, h_recv_sem, y_send, y_recv, z_send, z_recv, r_send, r_recv,
):
    ep_size = lax.axis_size("ep")
    groups = lax.axis_size("dp")
    count = tok_hbm.shape[0]
    col = tc.shape[3]
    tiles, _, rows, ft = h_own.shape
    nz = ep_size // 2
    half = rows // 2
    ep = lax.axis_index("ep")
    dp = lax.axis_index("dp")
    z, y = ep // 2, ep % 2
    xx, core = dp // 2, dp % 2
    mine = y * nz + z
    ynb = z * 2 + 1 - y
    peers_dp = (xx * 2 + 1 - core, (1 - xx) * 2 + core, (1 - xx) * 2 + 1 - core)
    f32 = jnp.float32
    bf16 = jnp.bfloat16

    def span(index, size):
        return pl.ds(pl.multiple_of(index * size, size), size)

    def remote(src, dst, send, recv, ep_to, dp_to):
        return pltpu.make_async_remote_copy(
            src_ref=src, dst_ref=dst, send_sem=send, recv_sem=recv,
            device_id=(ep_to, dp_to), device_id_type=pl.DeviceIdType.MESH,
        )

    loads = [
        pltpu.make_async_copy(ref.at[:, pl.ds(j * col, col)], tc.at[k, j, span(mine, count)], l_sem.at[k, j])
        for k, ref in enumerate((tok_hbm, cot_hbm))
        for j in range(groups)
    ]
    for load in loads:
        load.start()
    own_w = pltpu.make_async_copy(wd_ref.at[ep], wbuf.at[mine], l_sem.at[2, 0])
    own_w.start()
    w_loads = [
        pltpu.make_async_copy(src, dst, l_sem.at[2, 1 + k])
        for k, (src, dst) in enumerate(((wg_hbm, wg), (wu_hbm, wu), (wdn_hbm, wdn)))
    ]

    barrier = pltpu.get_barrier_semaphore()
    for k in range(1, ep_size):
        pl.semaphore_signal(
            barrier, inc=1, device_id=((ep + k) % ep_size, dp), device_id_type=pl.DeviceIdType.MESH
        )
    for peer in peers_dp:
        pl.semaphore_signal(barrier, inc=1, device_id=(ep, peer), device_id_type=pl.DeviceIdType.MESH)
    pl.semaphore_wait(barrier, ep_size - 1 + len(peers_dp))

    pending = []

    def go(copy):
        copy.start()
        pending.append(copy)

    def block(which, pos):
        return tc.at[which, :, span(pos, count)]

    def send_block(which, pos, ep_to, slot):
        go(remote(block(which, pos), block(which, pos), g_send.at[which, slot], g_recv.at[which, pos], ep_to, dp))

    def wait_block(which, pos):
        remote(block(which, pos), block(which, pos), g_send.at[which, 0], g_recv.at[which, pos], ep, dp).wait_recv()

    def send_cols(which, pos):
        for r, peer in enumerate(peers_dp):
            remote(
                tc.at[which, peer, span(pos, count)],
                cols.at[which, r, span(pos, count)],
                c_send.at[which, r], c_recv.at[which, r], ep, peer,
            ).start()

    for load in loads[:groups]:
        load.wait()
    for k in range(1, nz):
        send_block(0, mine, ((z + k) % nz) * 2 + y, k - 1)
    send_block(0, mine, ynb, nz - 1)
    for load in loads[groups:]:
        load.wait()
    for k in range(1, nz):
        send_block(1, mine, ((z + k) % nz) * 2 + y, k - 1)
    send_block(1, mine, ynb, nz - 1)
    for k in range(1, ep_size):
        to = (ep + k) % ep_size
        go(remote(wd_ref.at[to], wbuf.at[mine], w_send.at[k], w_recv.at[mine], to, dp))
    for load in w_loads:
        load.start()
    send_cols(0, mine)
    for k in range(1, nz):
        pos = y * nz + (z + k) % nz
        wait_block(0, pos)
        send_block(0, pos, ynb, nz - 1 + k)
        send_cols(0, pos)
    for k in range(nz):
        pos = (1 - y) * nz + (z + k) % nz
        wait_block(0, pos)
        send_cols(0, pos)
    send_cols(1, mine)
    for k in range(1, nz):
        pos = y * nz + (z + k) % nz
        wait_block(1, pos)
        send_block(1, pos, ynb, nz - 1 + k)
        send_cols(1, pos)
    own_w.wait()
    for k in range(1, ep_size):
        frm = (ep + k) % ep_size
        pos = (frm % 2) * nz + frm // 2
        remote(wd_ref.at[frm], wbuf.at[pos], w_send.at[k], w_recv.at[pos], ep, dp).wait_recv()
    for load in w_loads:
        load.wait()
    for k in range(nz):
        pos = (1 - y) * nz + (z + k) % nz
        wait_block(1, pos)
        send_cols(1, pos)

    weight = wbuf[...].reshape(rows, wbuf.shape[2])[:, 0:1]

    def tile_step(t, route):
        lanes = span(t, ft)
        gate_pre = jnp.zeros((rows, ft), f32)
        up_pre = jnp.zeros((rows, ft), f32)
        back = jnp.zeros((rows, ft), f32)
        for j in range(groups):
            depth = pl.ds(j * col, col)
            gate_pre += jnp.dot(tc[0, j], wg[depth, lanes], preferred_element_type=f32)
            up_pre += jnp.dot(tc[0, j], wu[depth, lanes], preferred_element_type=f32)
            back += lax.dot_general(tc[1, j], wdn[lanes, depth], contract_last, preferred_element_type=f32)
        act, slope = silu_parts(gate_pre)
        product = act * up_pre
        scaled = weight * back
        h_own[t, 0] = (scaled * up_pre * slope).astype(bf16)
        h_own[t, 1] = (scaled * act).astype(bf16)
        h_own[t, 2] = (weight * product).astype(bf16)
        route = route + jnp.sum(product.astype(bf16).astype(f32) * back, axis=1, keepdims=True)
        for r in (1, 0):
            remote(
                h_own.at[t], h_recv.at[r, t], h_send.at[r, t], h_recv_sem.at[r, t], ep, peers_dp[r]
            ).start()
        return route

    route = lax.fori_loop(0, tiles, tile_step, jnp.zeros((rows, 1), f32))
    rs[...] = jnp.broadcast_to(route, (rows, rs.shape[2])).reshape(rs.shape)

    def slot_step(n, carry):
        total = jnp.zeros((rows, col), f32)
        for t in range(tiles):
            lanes = pl.ds(t * ft, ft)
            total += lax.dot_general(h_own[t, 0], wg[span(n, col), lanes], contract_last, preferred_element_type=f32)
            total += lax.dot_general(h_own[t, 1], wu[span(n, col), lanes], contract_last, preferred_element_type=f32)
        part[n] = total.reshape(2, half, col)
        ys[n] = part[n, 1 - y].astype(bf16)
        remote(ys.at[n], yr.at[n], y_send.at[n], y_recv.at[n], ynb, dp).start()
        return carry

    lax.fori_loop(0, groups, slot_step, 0)
    for k in range(1, ep_size):
        to = (ep + k) % ep_size
        pos = (to % 2) * nz + to // 2
        go(remote(rs.at[pos], rr.at[ep], r_send.at[k], r_recv.at[ep], to, dp))

    colst[0] = tc[0, dp].T
    for r in range(3):
        remote(cols.at[0, r], cols.at[0, r], c_send.at[0, r], c_recv.at[0, r], ep, peers_dp[r]).wait_recv()
        colst[1 + r] = cols[0, r].T

    def forward(t):
        remote(h_own.at[t], h_recv.at[1, t], h_send.at[1, t], h_recv_sem.at[1, t], ep, peers_dp[1]).wait_recv()
        remote(
            h_recv.at[1, t], h_recv.at[2, t], h_send.at[2, t], h_recv_sem.at[2, t], ep, peers_dp[0]
        ).start()

    def add_step(n, carry):
        remote(ys.at[n], yr.at[n], y_send.at[n], y_recv.at[n], ynb, dp).wait()
        total = part[n, y] + yr[n].astype(f32)
        part[n, y] = total
        zs[n] = total.astype(bf16)
        for k in range(1, nz):
            to = (z + k) % nz
            remote(
                zs.at[n, span(to, count)], zr.at[n, k - 1], z_send.at[n, k - 1], z_recv.at[n, k - 1], to * 2 + y, dp
            ).start()
        return carry

    lax.fori_loop(0, groups, add_step, 0)
    forward(0)
    for r in range(3):
        remote(cols.at[1, r], cols.at[1, r], c_send.at[1, r], c_recv.at[1, r], ep, peers_dp[r]).wait_recv()

    def sum_step(n, carry):
        total = part[n, y, span(z, count), :]
        for k in range(1, nz):
            remote(
                zs.at[n, pl.ds(0, count)], zr.at[n, k - 1], z_send.at[n, k - 1], z_recv.at[n, k - 1], ep, dp
            ).wait()
            total = total + zr[n, k - 1].astype(f32)
        gt_ref[:, span(n, col)] = total.astype(bf16)
        return carry

    def weight_step(t, carry):
        @pl.when(t + 1 < tiles)
        def _():
            forward(t + 1)

        @pl.when(t + 1 == tiles)
        def _():
            lax.fori_loop(0, groups, sum_step, 0)

        for r in (0, 2):
            remote(h_own.at[t], h_recv.at[r, t], h_send.at[r, t], h_recv_sem.at[r, t], ep, peers_dp[0]).wait_recv()
        blocks = [h_own.at[t]] + [h_recv.at[r, t] for r in range(3)]
        cots = [tc.at[1, dp]] + [cols.at[1, r] for r in range(3)]
        grad_gate = jnp.zeros((col, ft), f32)
        grad_up = jnp.zeros((col, ft), f32)
        grad_down = jnp.zeros((ft, col), f32)
        for g in range(4):
            grad_gate += jnp.dot(colst[g], blocks[g][0], preferred_element_type=f32)
            grad_up += jnp.dot(colst[g], blocks[g][1], preferred_element_type=f32)
            grad_down += lax.dot_general(blocks[g][2], cots[g][...], contract_first, preferred_element_type=f32)
        gg_ref[:, span(t, ft)] = grad_gate.astype(bf16)
        gu_ref[:, span(t, ft)] = grad_up.astype(bf16)
        gd_ref[span(t, ft), :] = grad_down.astype(bf16)
        return carry

    lax.fori_loop(0, tiles, weight_step, 0)

    for k in range(1, ep_size):
        frm = (ep + k) % ep_size
        remote(rs.at[0], rr.at[frm], r_send.at[k], r_recv.at[frm], ep, dp).wait_recv()
        route_ref[frm] = rr[frm]
    route_ref[ep] = rs[mine]
    for copy in pending:
        copy.wait_send()
    for which in range(2):
        for r in range(3):
            remote(cols.at[which, r], cols.at[which, r], c_send.at[which, r], c_recv.at[which, r], ep, peers_dp[r]).wait_send()
    for t in range(tiles):
        for r in range(3):
            remote(h_own.at[t], h_recv.at[r, t], h_send.at[r, t], h_recv_sem.at[r, t], ep, peers_dp[r]).wait_send()


def fused_body(tokens, cotangent, expert_ids, route_weights, w_gate, w_up, w_down):
    count, topk = expert_ids.shape
    model = tokens.shape[1]
    experts = lax.axis_size("ep")
    groups = lax.axis_size("dp")
    width = w_gate.shape[2]
    rows = experts * count
    col = model // groups
    ft = 256 if width % 256 == 0 else width
    tiles = width // ft
    lanes = 128
    bf16 = jnp.bfloat16
    weights = dense_weights(expert_ids, route_weights, experts)
    spread = jnp.broadcast_to(weights.T[:, :, None], (experts, count, lanes))
    any_spec = pl.BlockSpec(memory_space=pl.ANY)
    vmem = pl.BlockSpec(memory_space=pltpu.VMEM)
    dma = pltpu.SemaphoreType.DMA
    nz = experts // 2
    outs = pl.pallas_call(
        fused_kernel,
        name="fused_layer",
        out_shape=(
            jax.ShapeDtypeStruct((count, model), bf16),
            jax.ShapeDtypeStruct((experts, count, lanes), jnp.float32),
            jax.ShapeDtypeStruct((col, width), bf16),
            jax.ShapeDtypeStruct((col, width), bf16),
            jax.ShapeDtypeStruct((width, col), bf16),
        ),
        in_specs=[any_spec, any_spec, vmem, any_spec, any_spec, any_spec],
        out_specs=(vmem,) * 5,
        scratch_shapes=[
            pltpu.VMEM((model, width), bf16),
            pltpu.VMEM((model, width), bf16),
            pltpu.VMEM((width, model), bf16),
            pltpu.VMEM((2, groups, rows, col), bf16),
            pltpu.VMEM((experts, count, lanes), jnp.float32),
            pltpu.VMEM((2, 3, rows, col), bf16),
            pltpu.VMEM((4, col, rows), bf16),
            pltpu.VMEM((tiles, 3, rows, ft), bf16),
            pltpu.VMEM((3, tiles, 3, rows, ft), bf16),
            pltpu.VMEM((groups, 2, rows // 2, col), jnp.float32),
            pltpu.VMEM((groups, rows // 2, col), bf16),
            pltpu.VMEM((groups, rows // 2, col), bf16),
            pltpu.VMEM((groups, rows // 2, col), bf16),
            pltpu.VMEM((groups, nz - 1, count, col), bf16),
            pltpu.VMEM((experts, count, lanes), jnp.float32),
            pltpu.VMEM((experts, count, lanes), jnp.float32),
            dma((3, max(groups, 4))),
            dma((experts,)),
            dma((experts,)),
            dma((2, 2 * nz)),
            dma((2, experts)),
            dma((2, 3)),
            dma((2, 3)),
            dma((3, tiles)),
            dma((3, tiles)),
            dma((groups,)),
            dma((groups,)),
            dma((groups, nz - 1)),
            dma((groups, nz - 1)),
            dma((experts,)),
            dma((experts,)),
        ],
        compiler_params=pltpu.CompilerParams(
            collective_id=0, has_side_effects=True, vmem_limit_bytes=60 * 1024 * 1024
        ),
    )(tokens, cotangent, spread, w_gate[0], w_up[0], w_down[0])
    grad_tokens, table, grad_gate, grad_up, grad_down = outs
    grad_route = pick_route(table[:, :, 0], expert_ids)
    return grad_tokens, grad_route, grad_gate[None], grad_up[None], grad_down[None]


def body(tokens, cotangent, expert_ids, route_weights, w_gate, w_up, w_down):
    tok_count, topk = expert_ids.shape
    experts = lax.axis_size("ep")
    whole = 2 * tok_count * topk // experts >= tok_count
    paired = lax.axis_size("dp") == 4 and experts % 2 == 0 and tok_count % 16 == 0
    chosen = fused_body if whole and paired else routed_body
    return chosen(tokens, cotangent, expert_ids, route_weights, w_gate, w_up, w_down)


def solution(mesh):
    return jax.shard_map(
        body,
        mesh=mesh,
        in_specs=(
            P(("ep", "dp"), None),
            P(("ep", "dp"), None),
            P(("ep", "dp"), None),
            P(("ep", "dp"), None),
            P("ep", None, None),
            P("ep", None, None),
            P("ep", None, None),
        ),
        out_specs=(
            P(("ep", "dp"), None),
            P(("ep", "dp"), None),
            P("ep", "dp", None),
            P("ep", "dp", None),
            P("ep", None, "dp"),
        ),
        check_vma=False,
    )
```

```python
import jax
import jax.numpy as jnp
from jax import lax
from jax.experimental import pallas as pl
from jax.experimental.pallas import tpu as pltpu
from jax.sharding import PartitionSpec as P

block_rows = 128
contract_last = (((1,), (1,)), ((), ()))
contract_first = (((0,), (0,)), ((), ()))


def silu_parts(gate_pre):
    sig = jax.nn.sigmoid(gate_pre)
    return (gate_pre * sig, sig * (1.0 + gate_pre * (1.0 - sig)))


def expert_pass(rows_x, rows_cot, rows_w, live_count, w_gate_one, w_up_one, w_down_one):
    total, model = rows_x.shape
    width = w_gate_one.shape[1]

    def step(index, carry):
        acc_gate, acc_up, acc_down, slot_grad, route_grad = carry
        start = index * block_rows
        tok = lax.dynamic_slice_in_dim(rows_x, start, block_rows, 0)
        cot = lax.dynamic_slice_in_dim(rows_cot, start, block_rows, 0)
        weight = lax.dynamic_slice_in_dim(rows_w, start, block_rows, 0).astype(jnp.float32)[:, None]
        gate_pre = jnp.dot(tok, w_gate_one, preferred_element_type=jnp.float32)
        up_pre = jnp.dot(tok, w_up_one, preferred_element_type=jnp.float32)
        act, slope = silu_parts(gate_pre)
        hidden = lax.optimization_barrier((act * up_pre).astype(jnp.bfloat16))
        back = lax.dot_general(cot, w_down_one, contract_last, preferred_element_type=jnp.float32)
        route_part = jnp.sum(hidden.astype(jnp.float32) * back, axis=1)
        scaled = weight * back
        grad_gate_pre = (scaled * up_pre * slope).astype(jnp.bfloat16)
        grad_up_pre = (scaled * act).astype(jnp.bfloat16)
        scaled_cot = (weight * cot.astype(jnp.float32)).astype(jnp.bfloat16)
        part = lax.dot_general(
            grad_gate_pre, w_gate_one, contract_last, preferred_element_type=jnp.float32
        )
        part = part + lax.dot_general(
            grad_up_pre, w_up_one, contract_last, preferred_element_type=jnp.float32
        )
        acc_gate = acc_gate + lax.dot_general(
            tok, grad_gate_pre, contract_first, preferred_element_type=jnp.float32
        )
        acc_up = acc_up + lax.dot_general(
            tok, grad_up_pre, contract_first, preferred_element_type=jnp.float32
        )
        acc_down = acc_down + lax.dot_general(
            hidden, scaled_cot, contract_first, preferred_element_type=jnp.float32
        )
        slot_grad = lax.dynamic_update_slice_in_dim(slot_grad, part, start, 0)
        route_grad = lax.dynamic_update_slice_in_dim(route_grad, route_part, start, 0)
        return (acc_gate, acc_up, acc_down, slot_grad, route_grad)

    init = (
        jnp.zeros((model, width), jnp.float32),
        jnp.zeros((model, width), jnp.float32),
        jnp.zeros((width, model), jnp.float32),
        jnp.zeros((total, model), jnp.float32),
        jnp.zeros((total,), jnp.float32),
    )
    block_count = (live_count + block_rows - 1) // block_rows
    return lax.fori_loop(0, block_count, step, init)


def routed_body(tokens, cotangent, expert_ids, route_weights, w_gate, w_up, w_down):
    tok_count, topk = expert_ids.shape
    model = tokens.shape[1]
    experts = lax.axis_size("ep")
    capacity = min(tok_count, 2 * tok_count * topk // experts)
    slots = tok_count * topk
    row_total = experts * capacity
    flat_ids = expert_ids.reshape(slots)
    onehot = (flat_ids[:, None] == jnp.arange(experts, dtype=jnp.int32)[None, :]).astype(jnp.int32)
    position = jnp.sum((jnp.cumsum(onehot, axis=0) - 1) * onehot, axis=1)
    slot_ids = jnp.arange(slots, dtype=jnp.int32)
    source = (
        jnp.full((row_total,), slots, jnp.int32).at[flat_ids * capacity + position].set(slot_ids)
    )
    filled = source < slots
    source_token = jnp.where(filled, source // topk, tok_count)
    joined = jnp.concatenate([tokens, cotangent], axis=1)
    picked = jnp.take(joined, source_token, axis=0, mode="fill", fill_value=0)
    send_x = picked[:, :model].reshape(experts, capacity, model)
    send_cot = picked[:, model:].reshape(experts, capacity, model)
    send_w = jnp.take(
        route_weights.reshape(slots), jnp.where(filled, source, slots), mode="fill", fill_value=0
    ).reshape(experts, capacity)
    recv_x, recv_cot, recv_w = (
        lax.all_to_all(send_x, "ep", split_axis=0, concat_axis=0, tiled=True),
        lax.all_to_all(send_cot, "ep", split_axis=0, concat_axis=0, tiled=True),
        lax.all_to_all(send_w, "ep", split_axis=0, concat_axis=0, tiled=True),
    )
    flat_w = recv_w.reshape(row_total)
    live = (flat_w != 0).astype(jnp.int32)
    live_count = jnp.sum(live)
    place = jnp.where(live > 0, jnp.cumsum(live) - 1, row_total)
    anchor = (
        jnp.full((row_total,), row_total, jnp.int32)
        .at[place]
        .set(jnp.arange(row_total, dtype=jnp.int32), mode="drop")
    )
    recv_joined = jnp.concatenate(
        [recv_x.reshape(row_total, model), recv_cot.reshape(row_total, model)], axis=1
    )
    packed = jnp.take(recv_joined, anchor, axis=0, mode="fill", fill_value=0)
    pack_x = packed[:, :model]
    pack_cot = packed[:, model:]
    pack_w = jnp.take(flat_w, anchor, mode="fill", fill_value=0)
    w_gate_one = w_gate[0]
    w_up_one = w_up[0]
    w_down_one = w_down[0]
    acc_gate, acc_up, acc_down, slot_grad, route_grad = expert_pass(
        pack_x, pack_cot, pack_w, live_count, w_gate_one, w_up_one, w_down_one
    )
    slot_rows = jnp.take(slot_grad, place, axis=0, mode="fill", fill_value=0.0).astype(jnp.bfloat16)
    route_rows = jnp.take(route_grad, place, axis=0, mode="fill", fill_value=0.0).astype(
        jnp.bfloat16
    )
    back_x, back_route_rows = (
        lax.all_to_all(
            slot_rows.reshape(experts, capacity, model),
            "ep",
            split_axis=0,
            concat_axis=0,
            tiled=True,
        ),
        lax.all_to_all(
            route_rows.reshape(experts, capacity), "ep", split_axis=0, concat_axis=0, tiled=True
        ),
    )
    mine_rows = back_x[flat_ids, position].reshape(tok_count, topk, model)
    grad_tokens = jnp.sum(mine_rows.astype(jnp.float32), axis=1).astype(jnp.bfloat16)
    grad_route = back_route_rows[flat_ids, position].reshape(tok_count, topk)
    summed = (
        lax.psum_scatter(
            acc_gate[None].astype(jnp.bfloat16), "dp", scatter_dimension=1, tiled=True
        ).astype(jnp.float32),
        lax.psum_scatter(
            acc_up[None].astype(jnp.bfloat16), "dp", scatter_dimension=1, tiled=True
        ).astype(jnp.float32),
        lax.psum_scatter(
            acc_down[None].astype(jnp.bfloat16), "dp", scatter_dimension=2, tiled=True
        ).astype(jnp.float32),
    )
    return (
        grad_tokens,
        grad_route,
        summed[0].astype(jnp.bfloat16),
        summed[1].astype(jnp.bfloat16),
        summed[2].astype(jnp.bfloat16),
    )


def fused_kernel(
    tok_hbm, cot_hbm, ids_ref, rw_ref, wg_hbm, wu_hbm, wdn_hbm,
    gt_ref, route_ref, gg_ref, gu_ref, gd_ref,
    wg, wu, wdn, tc, wd, wbuf, cols, colst, act_buf, fac_buf, hid_buf, hw_own, hw_recv, gp_own, gp_recv,
    part, ys, yr, zs, zr, rs, rr,
    l_sem, w_send, w_recv, g_send, g_recv, c_send, c_recv,
    h_send, h_done, y_send, y_recv, z_send, z_recv, r_send, r_recv,
):
    ep_size = lax.axis_size("ep")
    groups = lax.axis_size("dp")
    count = tok_hbm.shape[0]
    col = tc.shape[3]
    tiles, rows, ft = hw_own.shape
    nz = ep_size // 2
    half = rows // 2
    ep = lax.axis_index("ep")
    dp = lax.axis_index("dp")
    z, y = ep // 2, ep % 2
    xx, core = dp // 2, dp % 2
    mine = y * nz + z
    ynb = z * 2 + 1 - y
    peers_dp = (xx * 2 + 1 - core, (1 - xx) * 2 + core, (1 - xx) * 2 + 1 - core)
    f32 = jnp.float32
    bf16 = jnp.bfloat16

    def span(index, size):
        return pl.ds(pl.multiple_of(index * size, size), size)

    def remote(src, dst, send, recv, ep_to, dp_to):
        return pltpu.make_async_remote_copy(
            src_ref=src, dst_ref=dst, send_sem=send, recv_sem=recv,
            device_id=(ep_to, dp_to), device_id_type=pl.DeviceIdType.MESH,
        )

    loads = [
        pltpu.make_async_copy(ref.at[:, pl.ds(j * col, col)], tc.at[k, j, span(mine, count)], l_sem.at[k, j])
        for k, ref in enumerate((tok_hbm, cot_hbm))
        for j in range(groups)
    ]
    for load in loads:
        load.start()
    w_loads = [
        pltpu.make_async_copy(src, dst, l_sem.at[2, 1 + k])
        for k, (src, dst) in enumerate(((wg_hbm, wg), (wu_hbm, wu), (wdn_hbm, wdn)))
    ]

    barrier = pltpu.get_barrier_semaphore()
    for k in range(1, ep_size):
        pl.semaphore_signal(
            barrier, inc=1, device_id=((ep + k) % ep_size, dp), device_id_type=pl.DeviceIdType.MESH
        )
    for peer in peers_dp:
        pl.semaphore_signal(barrier, inc=1, device_id=(ep, peer), device_id_type=pl.DeviceIdType.MESH)
    wd[...] = jnp.zeros(wd.shape, f32)
    rs[...] = jnp.zeros(rs.shape, f32)
    ids = ids_ref[...]
    values = rw_ref[...].astype(f32)
    for e in range(ep_size):
        line = jnp.sum(jnp.where(ids == e, values, 0.0), axis=0, keepdims=True)
        wd[e, :, 0:count] = jnp.broadcast_to(line, (wd.shape[1], count))
    pl.semaphore_wait(barrier, ep_size - 1 + len(peers_dp))

    def block(which, zz, yy):
        return tc.at[which, :, span(yy * nz + zz, count)]

    def block_copy(which, way, zz, ep_to):
        view = block(which, zz, y)
        return remote(view, view, g_send.at[which, way, zz], g_recv.at[which, y * nz + zz], ep_to, dp)

    def send_up(which, zz):
        @pl.when(z + 1 < nz)
        def _():
            block_copy(which, 0, zz, ep + 2).start()

    def send_down(which, zz):
        @pl.when(z > 0)
        def _():
            block_copy(which, 1, zz, ep - 2).start()

    def send_side(which, zz):
        block_copy(which, 2, zz, ynb).start()

    def send_cols(which, pos):
        for r, peer in enumerate(peers_dp):
            remote(
                tc.at[which, peer, span(pos, count)],
                cols.at[which, r, span(pos, count)],
                c_send.at[which, r], c_recv.at[which, r], ep, peer,
            ).start()

    def pass_on(which, d):
        @pl.when(z >= d)
        def _():
            block_copy(which, 0, z - d, ep).wait_recv()
            send_up(which, z - d)
            send_side(which, z - d)
            send_cols(which, y * nz + z - d)

        @pl.when(z + d < nz)
        def _():
            block_copy(which, 1, z + d, ep).wait_recv()
            send_down(which, z + d)
            send_side(which, z + d)
            send_cols(which, y * nz + z + d)

    def take_side(which):
        def take(k, carry):
            zz = (z + k) % nz
            pos = (1 - y) * nz + zz
            view = tc.at[which, :, span(pos, count)]
            remote(view, view, g_send.at[which, 2, zz], g_recv.at[which, pos], ep, dp).wait_recv()
            send_cols(which, pos)
            return carry

        lax.fori_loop(0, nz, take, 0)

    def h_copy(kind, r, t, forwarded=False):
        own, got = ((hw_own, hw_recv), (gp_own, gp_recv))[kind]
        src = got.at[1, t] if forwarded else own.at[t]
        peer = peers_dp[0] if forwarded else peers_dp[r]
        return remote(src, got.at[r, t], h_send.at[kind, r, t], h_done.at[kind, r, t], ep, peer)

    def forward(kind, t):
        h_copy(kind, 1, t).wait_recv()
        h_copy(kind, 2, t, True).start()

    for which in range(2):
        for load in loads[which * groups:(which + 1) * groups]:
            load.wait()
        send_up(which, z)
        send_down(which, z)
        send_side(which, z)
        if which == 0:
            send_cols(0, mine)
    wbuf[mine] = wd[ep]
    for k in range(1, ep_size):
        to = (ep + k) % ep_size
        remote(wd.at[to], wbuf.at[mine], w_send.at[k], w_recv.at[mine], to, dp).start()
    for load in w_loads:
        load.start()
    for d in range(1, nz):
        pass_on(0, d)
    take_side(0)
    for k in range(1, ep_size):
        frm = (ep + k) % ep_size
        pos = (frm % 2) * nz + frm // 2
        remote(wd.at[frm], wbuf.at[pos], w_send.at[k], w_recv.at[pos], ep, dp).wait_recv()
    for load in w_loads:
        load.wait()
    flat = wbuf[...].reshape(ep_size * wbuf.shape[1], wbuf.shape[2])
    turned = jnp.concatenate([flat] * (128 // flat.shape[0]), axis=0).T
    step = wbuf.shape[1]
    weight = jnp.concatenate([turned[0:count, p * step:p * step + 1] for p in range(ep_size)], axis=0)

    for t in range(max(tiles, nz - 1)):
        if t < nz - 1:
            pass_on(1, t + 1)
        if t == 0:
            send_cols(1, mine)
        if t < tiles:
            lanes = pl.ds(t * ft, ft)
            gate_pre = jnp.zeros((rows, ft), f32)
            up_pre = jnp.zeros((rows, ft), f32)
            for j in range(groups):
                depth = pl.ds(j * col, col)
                gate_pre += jnp.dot(tc[0, j], wg[depth, lanes], preferred_element_type=f32)
                up_pre += jnp.dot(tc[0, j], wu[depth, lanes], preferred_element_type=f32)
            act, slope = silu_parts(gate_pre)
            product = act * up_pre
            hw_own[t] = (weight * product).astype(bf16)
            act_buf[t] = act
            fac_buf[t] = up_pre * slope
            hid_buf[t] = product.astype(bf16)
            for r in (1, 0):
                h_copy(0, r, t).start()
    take_side(1)

    def back_step(t, route):
        back = jnp.zeros((rows, ft), f32)
        for j in range(groups):
            back += lax.dot_general(
                tc[1, j], wdn[span(t, ft), pl.ds(j * col, col)], contract_last, preferred_element_type=f32
            )
        scaled = weight * back
        gp_own[t, 0] = (scaled * fac_buf[t]).astype(bf16)
        gp_own[t, 1] = (scaled * act_buf[t]).astype(bf16)
        route = route + jnp.sum(hid_buf[t].astype(f32) * back, axis=1, keepdims=True)
        for r in (1, 0):
            h_copy(1, r, t).start()
        return route

    route = lax.fori_loop(0, tiles, back_step, jnp.zeros((rows, 1), f32))
    lined = jnp.broadcast_to(route, (rows, 128)).T
    for p in range(ep_size):
        line = lined[0:1, p * count:(p + 1) * count]
        rs[p, :, 0:count] = jnp.broadcast_to(line, (rs.shape[1], count))

    def slot_step(n, carry):
        total = jnp.zeros((rows, col), f32)
        for t in range(tiles):
            lanes = pl.ds(t * ft, ft)
            total += lax.dot_general(gp_own[t, 0], wg[span(n, col), lanes], contract_last, preferred_element_type=f32)
            total += lax.dot_general(gp_own[t, 1], wu[span(n, col), lanes], contract_last, preferred_element_type=f32)
        part[n] = total.reshape(2, half, col)
        ys[n] = part[n, 1 - y].astype(bf16)
        remote(ys.at[n], yr.at[n], y_send.at[n], y_recv.at[n], ynb, dp).start()
        return carry

    lax.fori_loop(0, groups, slot_step, 0)
    for k in range(1, ep_size):
        to = (ep + k) % ep_size
        pos = (to % 2) * nz + to // 2
        remote(rs.at[pos], rr.at[ep], r_send.at[k], r_recv.at[ep], to, dp).start()
    rr[ep] = rs[mine]
    for t in range(tiles):
        forward(0, t)

    def add_step(n, carry):
        remote(ys.at[n], yr.at[n], y_send.at[n], y_recv.at[n], ynb, dp).wait()
        total = part[n, y] + yr[n].astype(f32)
        part[n, y] = total
        zs[n] = total.astype(bf16)
        for k in range(1, nz):
            to = (z + k) % nz
            remote(
                zs.at[n, span(to, count)], zr.at[n, k - 1], z_send.at[n, k - 1], z_recv.at[n, k - 1], to * 2 + y, dp
            ).start()
        return carry

    lax.fori_loop(0, groups, add_step, 0)
    colst[0] = tc[0, dp].T
    for r in range(3):
        remote(cols.at[0, r], cols.at[0, r], c_send.at[0, r], c_recv.at[0, r], ep, peers_dp[r]).wait_recv()
        colst[1 + r] = cols[0, r].T
    for r in range(3):
        remote(cols.at[1, r], cols.at[1, r], c_send.at[1, r], c_recv.at[1, r], ep, peers_dp[r]).wait_recv()
    forward(1, 0)

    def down_step(t, carry):
        for r in (0, 2):
            h_copy(0, r, t).wait_recv()
        blocks = [hw_own.at[t]] + [hw_recv.at[r, t] for r in range(3)]
        cots = [tc.at[1, dp]] + [cols.at[1, r] for r in range(3)]
        grad_down = jnp.zeros((ft, col), f32)
        for g in range(4):
            grad_down += lax.dot_general(blocks[g][...], cots[g][...], contract_first, preferred_element_type=f32)
        gd_ref[span(t, ft), :] = grad_down.astype(bf16)
        return carry

    lax.fori_loop(0, tiles, down_step, 0)

    def sum_step(n, carry):
        total = part[n, y, span(z, count), :]
        for k in range(1, nz):
            remote(
                zs.at[n, pl.ds(0, count)], zr.at[n, k - 1], z_send.at[n, k - 1], z_recv.at[n, k - 1], ep, dp
            ).wait()
            total = total + zr[n, k - 1].astype(f32)
        gt_ref[:, span(n, col)] = total.astype(bf16)
        return carry

    def weight_step(t, carry):
        @pl.when(t + 1 < tiles)
        def _():
            forward(1, t + 1)

        @pl.when(t + 1 == tiles)
        def _():
            lax.fori_loop(0, groups, sum_step, 0)

        for r in (0, 2):
            h_copy(1, r, t).wait_recv()
        blocks = [gp_own.at[t]] + [gp_recv.at[r, t] for r in range(3)]
        grad_gate = jnp.zeros((col, ft), f32)
        grad_up = jnp.zeros((col, ft), f32)
        for g in range(4):
            grad_gate += jnp.dot(colst[g], blocks[g][0], preferred_element_type=f32)
            grad_up += jnp.dot(colst[g], blocks[g][1], preferred_element_type=f32)
        gg_ref[:, span(t, ft)] = grad_gate.astype(bf16)
        gu_ref[:, span(t, ft)] = grad_up.astype(bf16)
        return carry

    lax.fori_loop(0, tiles, weight_step, 0)

    for k in range(1, ep_size):
        frm = (ep + k) % ep_size
        remote(rs.at[0], rr.at[frm], r_send.at[k], r_recv.at[frm], ep, dp).wait()
        remote(wd.at[0], wbuf.at[mine], w_send.at[k], w_recv.at[mine], ep, dp).wait_send()
    table = jnp.zeros(ids.shape, f32)
    for e in range(ep_size):
        table = table + jnp.where(ids == e, rr[e, 0:1, 0:count], 0.0)
    route_ref[...] = table.astype(bf16)
    for which in range(2):
        for zz in range(nz):
            block_copy(which, 2, zz, ep).wait_send()

            @pl.when(jnp.logical_and(z >= zz, z + 1 < nz))
            def _():
                block_copy(which, 0, zz, ep).wait_send()

            @pl.when(jnp.logical_and(z <= zz, z > 0))
            def _():
                block_copy(which, 1, zz, ep).wait_send()

        for r in range(3):
            remote(cols.at[which, r], cols.at[which, r], c_send.at[which, r], c_recv.at[which, r], ep, peers_dp[r]).wait_send()
        for t in range(tiles):
            for r in range(3):
                h_copy(which, r, t).wait_send()


def store_kernel(*refs):
    sems = refs[-1]
    each = (len(refs) - 1) // 2
    copies = [pltpu.make_async_copy(refs[k], refs[each + k], sems.at[k]) for k in range(each)]
    for copy in copies:
        copy.start()
    for copy in copies:
        copy.wait()


def fused_body(tokens, cotangent, expert_ids, route_weights, w_gate, w_up, w_down):
    count, topk = expert_ids.shape
    model = tokens.shape[1]
    experts = lax.axis_size("ep")
    groups = lax.axis_size("dp")
    width = w_gate.shape[2]
    rows = experts * count
    col = model // groups
    ft = 256 if width % 256 == 0 else width
    tiles = width // ft
    lanes = 128
    bf16 = jnp.bfloat16
    f32 = jnp.float32
    any_spec = pl.BlockSpec(memory_space=pl.ANY)
    vmem = pl.BlockSpec(memory_space=pltpu.VMEM)
    dma = pltpu.SemaphoreType.DMA
    nz = experts // 2
    small = (experts, 8, lanes)
    shapes = ((count, model), (topk, count), (col, width), (col, width), (width, col))
    outs = pl.pallas_call(
        fused_kernel,
        name="fused_layer",
        out_shape=tuple(pltpu.VMEM(shape, bf16) for shape in shapes),
        in_specs=[any_spec, any_spec, vmem, vmem, any_spec, any_spec, any_spec],
        out_specs=(vmem,) * 5,
        scratch_shapes=[
            pltpu.VMEM((model, width), bf16),
            pltpu.VMEM((model, width), bf16),
            pltpu.VMEM((width, model), bf16),
            pltpu.VMEM((2, groups, rows, col), bf16),
            pltpu.VMEM(small, f32),
            pltpu.VMEM(small, f32),
            pltpu.VMEM((2, 3, rows, col), bf16),
            pltpu.VMEM((4, col, rows), bf16),
            pltpu.VMEM((tiles, rows, ft), f32),
            pltpu.VMEM((tiles, rows, ft), f32),
            pltpu.VMEM((tiles, rows, ft), bf16),
            pltpu.VMEM((tiles, rows, ft), bf16),
            pltpu.VMEM((3, tiles, rows, ft), bf16),
            pltpu.VMEM((tiles, 2, rows, ft), bf16),
            pltpu.VMEM((3, tiles, 2, rows, ft), bf16),
            pltpu.VMEM((groups, 2, rows // 2, col), f32),
            pltpu.VMEM((groups, rows // 2, col), bf16),
            pltpu.VMEM((groups, rows // 2, col), bf16),
            pltpu.VMEM((groups, rows // 2, col), bf16),
            pltpu.VMEM((groups, nz - 1, count, col), bf16),
            pltpu.VMEM(small, f32),
            pltpu.VMEM(small, f32),
            dma((3, max(groups, 4))),
            dma((experts,)),
            dma((experts,)),
            dma((2, 3, nz)),
            dma((2, experts)),
            dma((2, 3)),
            dma((2, 3)),
            dma((2, 3, tiles)),
            dma((2, 3, tiles)),
            dma((groups,)),
            dma((groups,)),
            dma((groups, nz - 1)),
            dma((groups, nz - 1)),
            dma((experts,)),
            dma((experts,)),
        ],
        compiler_params=pltpu.CompilerParams(
            collective_id=0, has_side_effects=True, vmem_limit_bytes=48 * 1024 * 1024
        ),
    )(tokens, cotangent, expert_ids.T, route_weights.T, w_gate[0], w_up[0], w_down[0])
    outs = pl.pallas_call(
        store_kernel,
        name="store_results",
        out_shape=tuple(jax.ShapeDtypeStruct(shape, bf16) for shape in shapes),
        in_specs=[vmem] * 5,
        out_specs=(any_spec,) * 5,
        scratch_shapes=[dma((5,))],
    )(*outs)
    grad_tokens, grad_route, grad_gate, grad_up, grad_down = outs
    return grad_tokens, grad_route.T, grad_gate[None], grad_up[None], grad_down[None]


def body(tokens, cotangent, expert_ids, route_weights, w_gate, w_up, w_down):
    tok_count, topk = expert_ids.shape
    experts = lax.axis_size("ep")
    whole = 2 * tok_count * topk // experts >= tok_count
    paired = lax.axis_size("dp") == 4 and experts in (4, 8, 16) and tok_count in (16, 32, 64, 128)
    chosen = fused_body if whole and paired else routed_body
    return chosen(tokens, cotangent, expert_ids, route_weights, w_gate, w_up, w_down)


def solution(mesh):
    return jax.shard_map(
        body,
        mesh=mesh,
        in_specs=(
            P(("ep", "dp"), None),
            P(("ep", "dp"), None),
            P(("ep", "dp"), None),
            P(("ep", "dp"), None),
            P("ep", None, None),
            P("ep", None, None),
            P("ep", None, None),
        ),
        out_specs=(
            P(("ep", "dp"), None),
            P(("ep", "dp"), None),
            P("ep", "dp", None),
            P("ep", "dp", None),
            P("ep", None, "dp"),
        ),
        check_vma=False,
    )
```

```python
import jax
import jax.numpy as jnp
from jax import lax
from jax.experimental import pallas as pl
from jax.experimental.pallas import tpu as pltpu
from jax.sharding import PartitionSpec as P

block_rows = 128
contract_last = (((1,), (1,)), ((), ()))
contract_first = (((0,), (0,)), ((), ()))


def silu_parts(gate_pre):
    sig = jax.nn.sigmoid(gate_pre)
    return (gate_pre * sig, sig * (1.0 + gate_pre * (1.0 - sig)))


def expert_pass(rows_x, rows_cot, rows_w, live_count, w_gate_one, w_up_one, w_down_one):
    total, model = rows_x.shape
    width = w_gate_one.shape[1]

    def step(index, carry):
        acc_gate, acc_up, acc_down, slot_grad, route_grad = carry
        start = index * block_rows
        tok = lax.dynamic_slice_in_dim(rows_x, start, block_rows, 0)
        cot = lax.dynamic_slice_in_dim(rows_cot, start, block_rows, 0)
        weight = lax.dynamic_slice_in_dim(rows_w, start, block_rows, 0).astype(jnp.float32)[:, None]
        gate_pre = jnp.dot(tok, w_gate_one, preferred_element_type=jnp.float32)
        up_pre = jnp.dot(tok, w_up_one, preferred_element_type=jnp.float32)
        act, slope = silu_parts(gate_pre)
        hidden = lax.optimization_barrier((act * up_pre).astype(jnp.bfloat16))
        back = lax.dot_general(cot, w_down_one, contract_last, preferred_element_type=jnp.float32)
        route_part = jnp.sum(hidden.astype(jnp.float32) * back, axis=1)
        scaled = weight * back
        grad_gate_pre = (scaled * up_pre * slope).astype(jnp.bfloat16)
        grad_up_pre = (scaled * act).astype(jnp.bfloat16)
        scaled_cot = (weight * cot.astype(jnp.float32)).astype(jnp.bfloat16)
        part = lax.dot_general(
            grad_gate_pre, w_gate_one, contract_last, preferred_element_type=jnp.float32
        )
        part = part + lax.dot_general(
            grad_up_pre, w_up_one, contract_last, preferred_element_type=jnp.float32
        )
        acc_gate = acc_gate + lax.dot_general(
            tok, grad_gate_pre, contract_first, preferred_element_type=jnp.float32
        )
        acc_up = acc_up + lax.dot_general(
            tok, grad_up_pre, contract_first, preferred_element_type=jnp.float32
        )
        acc_down = acc_down + lax.dot_general(
            hidden, scaled_cot, contract_first, preferred_element_type=jnp.float32
        )
        slot_grad = lax.dynamic_update_slice_in_dim(slot_grad, part, start, 0)
        route_grad = lax.dynamic_update_slice_in_dim(route_grad, route_part, start, 0)
        return (acc_gate, acc_up, acc_down, slot_grad, route_grad)

    init = (
        jnp.zeros((model, width), jnp.float32),
        jnp.zeros((model, width), jnp.float32),
        jnp.zeros((width, model), jnp.float32),
        jnp.zeros((total, model), jnp.float32),
        jnp.zeros((total,), jnp.float32),
    )
    block_count = (live_count + block_rows - 1) // block_rows
    return lax.fori_loop(0, block_count, step, init)


def routed_body(tokens, cotangent, expert_ids, route_weights, w_gate, w_up, w_down):
    tok_count, topk = expert_ids.shape
    model = tokens.shape[1]
    experts = lax.axis_size("ep")
    capacity = min(tok_count, 2 * tok_count * topk // experts)
    slots = tok_count * topk
    row_total = experts * capacity
    flat_ids = expert_ids.reshape(slots)
    onehot = (flat_ids[:, None] == jnp.arange(experts, dtype=jnp.int32)[None, :]).astype(jnp.int32)
    position = jnp.sum((jnp.cumsum(onehot, axis=0) - 1) * onehot, axis=1)
    slot_ids = jnp.arange(slots, dtype=jnp.int32)
    source = (
        jnp.full((row_total,), slots, jnp.int32).at[flat_ids * capacity + position].set(slot_ids)
    )
    filled = source < slots
    source_token = jnp.where(filled, source // topk, tok_count)
    joined = jnp.concatenate([tokens, cotangent], axis=1)
    picked = jnp.take(joined, source_token, axis=0, mode="fill", fill_value=0)
    send_x = picked[:, :model].reshape(experts, capacity, model)
    send_cot = picked[:, model:].reshape(experts, capacity, model)
    send_w = jnp.take(
        route_weights.reshape(slots), jnp.where(filled, source, slots), mode="fill", fill_value=0
    ).reshape(experts, capacity)
    recv_x, recv_cot, recv_w = (
        lax.all_to_all(send_x, "ep", split_axis=0, concat_axis=0, tiled=True),
        lax.all_to_all(send_cot, "ep", split_axis=0, concat_axis=0, tiled=True),
        lax.all_to_all(send_w, "ep", split_axis=0, concat_axis=0, tiled=True),
    )
    flat_w = recv_w.reshape(row_total)
    live = (flat_w != 0).astype(jnp.int32)
    live_count = jnp.sum(live)
    place = jnp.where(live > 0, jnp.cumsum(live) - 1, row_total)
    anchor = (
        jnp.full((row_total,), row_total, jnp.int32)
        .at[place]
        .set(jnp.arange(row_total, dtype=jnp.int32), mode="drop")
    )
    recv_joined = jnp.concatenate(
        [recv_x.reshape(row_total, model), recv_cot.reshape(row_total, model)], axis=1
    )
    packed = jnp.take(recv_joined, anchor, axis=0, mode="fill", fill_value=0)
    pack_x = packed[:, :model]
    pack_cot = packed[:, model:]
    pack_w = jnp.take(flat_w, anchor, mode="fill", fill_value=0)
    w_gate_one = w_gate[0]
    w_up_one = w_up[0]
    w_down_one = w_down[0]
    acc_gate, acc_up, acc_down, slot_grad, route_grad = expert_pass(
        pack_x, pack_cot, pack_w, live_count, w_gate_one, w_up_one, w_down_one
    )
    slot_rows = jnp.take(slot_grad, place, axis=0, mode="fill", fill_value=0.0).astype(jnp.bfloat16)
    route_rows = jnp.take(route_grad, place, axis=0, mode="fill", fill_value=0.0).astype(
        jnp.bfloat16
    )
    back_x, back_route_rows = (
        lax.all_to_all(
            slot_rows.reshape(experts, capacity, model),
            "ep",
            split_axis=0,
            concat_axis=0,
            tiled=True,
        ),
        lax.all_to_all(
            route_rows.reshape(experts, capacity), "ep", split_axis=0, concat_axis=0, tiled=True
        ),
    )
    mine_rows = back_x[flat_ids, position].reshape(tok_count, topk, model)
    grad_tokens = jnp.sum(mine_rows.astype(jnp.float32), axis=1).astype(jnp.bfloat16)
    grad_route = back_route_rows[flat_ids, position].reshape(tok_count, topk)
    summed = (
        lax.psum_scatter(
            acc_gate[None].astype(jnp.bfloat16), "dp", scatter_dimension=1, tiled=True
        ).astype(jnp.float32),
        lax.psum_scatter(
            acc_up[None].astype(jnp.bfloat16), "dp", scatter_dimension=1, tiled=True
        ).astype(jnp.float32),
        lax.psum_scatter(
            acc_down[None].astype(jnp.bfloat16), "dp", scatter_dimension=2, tiled=True
        ).astype(jnp.float32),
    )
    return (
        grad_tokens,
        grad_route,
        summed[0].astype(jnp.bfloat16),
        summed[1].astype(jnp.bfloat16),
        summed[2].astype(jnp.bfloat16),
    )


def fused_kernel(
    tok_hbm, cot_hbm, ids_hbm, rw_hbm, wg_hbm, wu_hbm, wdn_hbm,
    gt_ref, route_ref, gg_ref, gu_ref, gd_ref,
    ids_ref, rw_ref, wg, wu, wdn, tc, wd, wbuf, cols, colst, act_buf, fac_buf, hid_buf, hw_own, hw_recv, gp_own, gp_recv,
    part, ys, yr, zs, zr, rs, rr,
    l_sem, w_send, w_recv, g_send, g_recv, c_send, c_recv,
    h_send, h_done, y_send, y_recv, z_send, z_recv, r_send, r_recv,
):
    ep_size = lax.axis_size("ep")
    groups = lax.axis_size("dp")
    count = tok_hbm.shape[0]
    col = tc.shape[3]
    tiles, rows, ft = hw_own.shape
    nz = ep_size // 2
    half = rows // 2
    ep = lax.axis_index("ep")
    dp = lax.axis_index("dp")
    z, y = ep // 2, ep % 2
    xx, core = dp // 2, dp % 2
    mine = y * nz + z
    ynb = z * 2 + 1 - y
    peers_dp = (xx * 2 + 1 - core, (1 - xx) * 2 + core, (1 - xx) * 2 + 1 - core)
    f32 = jnp.float32
    bf16 = jnp.bfloat16

    def span(index, size):
        return pl.ds(pl.multiple_of(index * size, size), size)

    def remote(src, dst, send, recv, ep_to, dp_to):
        return pltpu.make_async_remote_copy(
            src_ref=src, dst_ref=dst, send_sem=send, recv_sem=recv,
            device_id=(ep_to, dp_to), device_id_type=pl.DeviceIdType.MESH,
        )

    loads = [
        pltpu.make_async_copy(ref.at[:, pl.ds(j * col, col)], tc.at[k, j, span(mine, count)], l_sem.at[k, j])
        for k, ref in enumerate((tok_hbm, cot_hbm))
        for j in range(groups)
    ]
    for load in loads:
        load.start()
    lists = (
        pltpu.make_async_copy(ids_hbm, ids_ref, l_sem.at[3, 0]),
        pltpu.make_async_copy(rw_hbm, rw_ref, l_sem.at[3, 1]),
    )
    for load in lists:
        load.start()
    w_loads = [
        pltpu.make_async_copy(src, dst, l_sem.at[2, 1 + k])
        for k, (src, dst) in enumerate(((wg_hbm, wg), (wu_hbm, wu), (wdn_hbm, wdn)))
    ]

    barrier = pltpu.get_barrier_semaphore()
    for k in range(1, ep_size):
        pl.semaphore_signal(
            barrier, inc=1, device_id=((ep + k) % ep_size, dp), device_id_type=pl.DeviceIdType.MESH
        )
    for peer in peers_dp:
        pl.semaphore_signal(barrier, inc=1, device_id=(ep, peer), device_id_type=pl.DeviceIdType.MESH)
    wd[...] = jnp.zeros(wd.shape, f32)
    rs[...] = jnp.zeros(rs.shape, f32)
    for load in lists:
        load.wait()
    ids = ids_ref[...]
    values = rw_ref[...].astype(f32)
    for e in range(ep_size):
        line = jnp.sum(jnp.where(ids == e, values, 0.0), axis=0, keepdims=True)
        wd[e, :, 0:count] = jnp.broadcast_to(line, (wd.shape[1], count))
    pl.semaphore_wait(barrier, ep_size - 1 + len(peers_dp))

    def block(which, zz, yy):
        if which == 2:
            return cols.at[1, pl.ds(1, 2), span(yy * nz + zz, count)]
        return tc.at[which, :, span(yy * nz + zz, count)]

    def block_copy(which, way, zz, ep_to):
        view = block(which, zz, y)
        return remote(view, view, g_send.at[which, way, zz], g_recv.at[which, y * nz + zz], ep_to, dp)

    def send_up(which, zz):
        @pl.when(z + 1 < nz)
        def _():
            block_copy(which, 0, zz, ep + 2).start()

    def send_down(which, zz):
        @pl.when(z > 0)
        def _():
            block_copy(which, 1, zz, ep - 2).start()

    def send_side(which, zz):
        block_copy(which, 2, zz, ynb).start()

    def send_cols(which, pos, reach=3):
        if which == 2:
            return
        for r, peer in enumerate(peers_dp[:reach]):
            remote(
                tc.at[which, peer, span(pos, count)],
                cols.at[which, r, span(pos, count)],
                c_send.at[which, r], c_recv.at[which, r], ep, peer,
            ).start()

    def pass_on(which, d):
        @pl.when(z >= d)
        def _():
            block_copy(which, 0, z - d, ep).wait_recv()
            send_up(which, z - d)
            send_side(which, z - d)
            send_cols(which, y * nz + z - d, 3 - 2 * which)

        @pl.when(z + d < nz)
        def _():
            block_copy(which, 1, z + d, ep).wait_recv()
            send_down(which, z + d)
            send_side(which, z + d)
            send_cols(which, y * nz + z + d, 3 - 2 * which)

    def take_side(which):
        def take(k, carry):
            zz = (z + k) % nz
            pos = (1 - y) * nz + zz
            view = block(which, zz, 1 - y)
            remote(view, view, g_send.at[which, 2, zz], g_recv.at[which, pos], ep, dp).wait_recv()
            send_cols(which, pos, 3 - 2 * which)
            return carry

        lax.fori_loop(0, nz, take, 0)

    def h_copy(kind, r, t, forwarded=False):
        own, got = ((hw_own, hw_recv), (gp_own, gp_recv))[kind]
        src = got.at[1, t] if forwarded else own.at[t]
        peer = peers_dp[0] if forwarded else peers_dp[r]
        return remote(src, got.at[r, t], h_send.at[kind, r, t], h_done.at[kind, r, t], ep, peer)

    def forward(kind, t):
        h_copy(kind, 1, t).wait_recv()
        h_copy(kind, 2, t, True).start()

    for which in range(2):
        for load in loads[which * groups:(which + 1) * groups]:
            load.wait()
        send_up(which, z)
        send_down(which, z)
        send_side(which, z)
        send_cols(which, mine)
    wbuf[mine] = wd[ep]
    for k in range(1, ep_size):
        to = (ep + k) % ep_size
        remote(wd.at[to], wbuf.at[mine], w_send.at[k], w_recv.at[mine], to, dp).start()
    for load in w_loads:
        load.start()
    for d in range(1, nz):
        pass_on(0, d)
    take_side(0)
    for k in range(1, ep_size):
        frm = (ep + k) % ep_size
        pos = (frm % 2) * nz + frm // 2
        remote(wd.at[frm], wbuf.at[pos], w_send.at[k], w_recv.at[pos], ep, dp).wait_recv()
    for load in w_loads:
        load.wait()
    flat = wbuf[...].reshape(ep_size * wbuf.shape[1], wbuf.shape[2])
    turned = jnp.concatenate([flat] * (128 // flat.shape[0]), axis=0).T
    step = wbuf.shape[1]
    weight = jnp.concatenate([turned[0:count, p * step:p * step + 1] for p in range(ep_size)], axis=0)

    for t in range(max(tiles, nz - 1)):
        if t < nz - 1:
            pass_on(1, t + 1)
        if t < tiles:
            lanes = pl.ds(t * ft, ft)
            gate_pre = jnp.zeros((rows, ft), f32)
            up_pre = jnp.zeros((rows, ft), f32)
            for j in range(groups):
                depth = pl.ds(j * col, col)
                gate_pre += jnp.dot(tc[0, j], wg[depth, lanes], preferred_element_type=f32)
                up_pre += jnp.dot(tc[0, j], wu[depth, lanes], preferred_element_type=f32)
            act, slope = silu_parts(gate_pre)
            product = act * up_pre
            hw_own[t] = (weight * product).astype(bf16)
            act_buf[t] = act
            fac_buf[t] = up_pre * slope
            hid_buf[t] = product.astype(bf16)
            for r in (1, 0):
                h_copy(0, r, t).start()
    for r in (1, 2):
        view = cols.at[1, r, span(mine, count)]
        remote(view, view, c_send.at[1, r], c_recv.at[1, r], ep, peers_dp[r]).wait_recv()
    send_up(2, z)
    send_down(2, z)
    take_side(1)
    send_side(2, z)
    pass_on(2, 1)

    def back_step(t, route):
        back = jnp.zeros((rows, ft), f32)
        for j in range(groups):
            back += lax.dot_general(
                tc[1, j], wdn[span(t, ft), pl.ds(j * col, col)], contract_last, preferred_element_type=f32
            )
        scaled = weight * back
        gp_own[t, 0] = (scaled * fac_buf[t]).astype(bf16)
        gp_own[t, 1] = (scaled * act_buf[t]).astype(bf16)
        route = route + jnp.sum(hid_buf[t].astype(f32) * back, axis=1, keepdims=True)
        for r in (1, 0):
            h_copy(1, r, t).start()
        return route

    route = lax.fori_loop(0, tiles, back_step, jnp.zeros((rows, 1), f32))
    for d in range(2, nz):
        pass_on(2, d)
    lined = jnp.broadcast_to(route, (rows, 128)).T
    for p in range(ep_size):
        line = lined[0:1, p * count:(p + 1) * count]
        rs[p, :, 0:count] = jnp.broadcast_to(line, (rs.shape[1], count))

    def slot_step(n, carry):
        total = jnp.zeros((rows, col), f32)
        for t in range(tiles):
            lanes = pl.ds(t * ft, ft)
            total += lax.dot_general(gp_own[t, 0], wg[span(n, col), lanes], contract_last, preferred_element_type=f32)
            total += lax.dot_general(gp_own[t, 1], wu[span(n, col), lanes], contract_last, preferred_element_type=f32)
        part[n] = total.reshape(2, half, col)
        ys[n] = part[n, 1 - y].astype(bf16)
        remote(ys.at[n], yr.at[n], y_send.at[n], y_recv.at[n], ynb, dp).start()
        return carry

    lax.fori_loop(0, groups, slot_step, 0)
    for k in range(1, ep_size):
        to = (ep + k) % ep_size
        pos = (to % 2) * nz + to // 2
        remote(rs.at[pos], rr.at[ep], r_send.at[k], r_recv.at[ep], to, dp).start()
    rr[ep] = rs[mine]
    for t in range(tiles):
        forward(0, t)

    def add_step(n, carry):
        remote(ys.at[n], yr.at[n], y_send.at[n], y_recv.at[n], ynb, dp).wait()
        total = part[n, y] + yr[n].astype(f32)
        part[n, y] = total
        zs[n] = total.astype(bf16)
        for k in range(1, nz):
            to = (z + k) % nz
            remote(
                zs.at[n, span(to, count)], zr.at[n, k - 1], z_send.at[n, k - 1], z_recv.at[n, k - 1], to * 2 + y, dp
            ).start()
        return carry

    lax.fori_loop(0, groups, add_step, 0)
    colst[0] = tc[0, dp].T
    for r in range(3):
        remote(cols.at[0, r], cols.at[0, r], c_send.at[0, r], c_recv.at[0, r], ep, peers_dp[r]).wait_recv()
        colst[1 + r] = cols[0, r].T
    remote(cols.at[1, 0], cols.at[1, 0], c_send.at[1, 0], c_recv.at[1, 0], ep, peers_dp[0]).wait_recv()
    take_side(2)
    forward(1, 0)

    def down_step(t, carry):
        for r in (0, 2):
            h_copy(0, r, t).wait_recv()
        blocks = [hw_own.at[t]] + [hw_recv.at[r, t] for r in range(3)]
        cots = [tc.at[1, dp]] + [cols.at[1, r] for r in range(3)]
        grad_down = jnp.zeros((ft, col), f32)
        for g in range(4):
            grad_down += lax.dot_general(blocks[g][...], cots[g][...], contract_first, preferred_element_type=f32)
        gd_ref[span(t, ft), :] = grad_down.astype(bf16)
        return carry

    lax.fori_loop(0, tiles, down_step, 0)

    def sum_step(n, carry):
        total = part[n, y, span(z, count), :]
        for k in range(1, nz):
            remote(
                zs.at[n, pl.ds(0, count)], zr.at[n, k - 1], z_send.at[n, k - 1], z_recv.at[n, k - 1], ep, dp
            ).wait()
            total = total + zr[n, k - 1].astype(f32)
        gt_ref[:, span(n, col)] = total.astype(bf16)
        return carry

    def weight_step(t, carry):
        @pl.when(t + 1 < tiles)
        def _():
            forward(1, t + 1)

        @pl.when(t + 1 == tiles)
        def _():
            lax.fori_loop(0, groups, sum_step, 0)

        for r in (0, 2):
            h_copy(1, r, t).wait_recv()
        blocks = [gp_own.at[t]] + [gp_recv.at[r, t] for r in range(3)]
        grad_gate = jnp.zeros((col, ft), f32)
        grad_up = jnp.zeros((col, ft), f32)
        for g in range(4):
            grad_gate += jnp.dot(colst[g], blocks[g][0], preferred_element_type=f32)
            grad_up += jnp.dot(colst[g], blocks[g][1], preferred_element_type=f32)
        gg_ref[:, span(t, ft)] = grad_gate.astype(bf16)
        gu_ref[:, span(t, ft)] = grad_up.astype(bf16)
        return carry

    lax.fori_loop(0, tiles, weight_step, 0)

    for k in range(1, ep_size):
        frm = (ep + k) % ep_size
        remote(rs.at[0], rr.at[frm], r_send.at[k], r_recv.at[frm], ep, dp).wait()
        remote(wd.at[0], wbuf.at[mine], w_send.at[k], w_recv.at[mine], ep, dp).wait_send()
    table = jnp.zeros(ids.shape, f32)
    for e in range(ep_size):
        table = table + jnp.where(ids == e, rr[e, 0:1, 0:count], 0.0)
    route_ref[...] = table.astype(bf16)
    for which in range(3):
        for zz in range(nz):
            block_copy(which, 2, zz, ep).wait_send()

            @pl.when(jnp.logical_and(z >= zz, z + 1 < nz))
            def _():
                block_copy(which, 0, zz, ep).wait_send()

            @pl.when(jnp.logical_and(z <= zz, z > 0))
            def _():
                block_copy(which, 1, zz, ep).wait_send()

    for which in range(2):
        for r in range(3):
            view = cols.at[1, r, span(mine, count)] if which == 1 and r > 0 else cols.at[which, r]
            remote(view, view, c_send.at[which, r], c_recv.at[which, r], ep, peers_dp[r]).wait_send()
        for t in range(tiles):
            for r in range(3):
                h_copy(which, r, t).wait_send()


def store_kernel(*refs):
    sems = refs[-1]
    each = (len(refs) - 1) // 2
    copies = [pltpu.make_async_copy(refs[k], refs[each + k], sems.at[k]) for k in range(each)]
    for copy in copies:
        copy.start()
    for copy in copies:
        copy.wait()


def fused_body(tokens, cotangent, expert_ids, route_weights, w_gate, w_up, w_down):
    count, topk = expert_ids.shape
    model = tokens.shape[1]
    experts = lax.axis_size("ep")
    groups = lax.axis_size("dp")
    width = w_gate.shape[2]
    rows = experts * count
    col = model // groups
    ft = 256 if width % 256 == 0 else width
    tiles = width // ft
    lanes = 128
    bf16 = jnp.bfloat16
    f32 = jnp.float32
    any_spec = pl.BlockSpec(memory_space=pl.ANY)
    hbm = pl.BlockSpec(memory_space=pltpu.HBM)
    vmem = pl.BlockSpec(memory_space=pltpu.VMEM)
    dma = pltpu.SemaphoreType.DMA
    nz = experts // 2
    small = (experts, 8, lanes)
    shapes = ((count, model), (topk, count), (col, width), (col, width), (width, col))
    outs = pl.pallas_call(
        fused_kernel,
        name="fused_layer",
        out_shape=tuple(pltpu.VMEM(shape, bf16) for shape in shapes),
        in_specs=[hbm] * 7,
        out_specs=(vmem,) * 5,
        scratch_shapes=[
            pltpu.VMEM((topk, count), jnp.int32),
            pltpu.VMEM((topk, count), bf16),
            pltpu.VMEM((model, width), bf16),
            pltpu.VMEM((model, width), bf16),
            pltpu.VMEM((width, model), bf16),
            pltpu.VMEM((2, groups, rows, col), bf16),
            pltpu.VMEM(small, f32),
            pltpu.VMEM(small, f32),
            pltpu.VMEM((2, 3, rows, col), bf16),
            pltpu.VMEM((4, col, rows), bf16),
            pltpu.VMEM((tiles, rows, ft), f32),
            pltpu.VMEM((tiles, rows, ft), f32),
            pltpu.VMEM((tiles, rows, ft), bf16),
            pltpu.VMEM((tiles, rows, ft), bf16),
            pltpu.VMEM((3, tiles, rows, ft), bf16),
            pltpu.VMEM((tiles, 2, rows, ft), bf16),
            pltpu.VMEM((3, tiles, 2, rows, ft), bf16),
            pltpu.VMEM((groups, 2, rows // 2, col), f32),
            pltpu.VMEM((groups, rows // 2, col), bf16),
            pltpu.VMEM((groups, rows // 2, col), bf16),
            pltpu.VMEM((groups, rows // 2, col), bf16),
            pltpu.VMEM((groups, nz - 1, count, col), bf16),
            pltpu.VMEM(small, f32),
            pltpu.VMEM(small, f32),
            dma((4, max(groups, 4))),
            dma((experts,)),
            dma((experts,)),
            dma((3, 3, nz)),
            dma((3, experts)),
            dma((2, 3)),
            dma((2, 3)),
            dma((2, 3, tiles)),
            dma((2, 3, tiles)),
            dma((groups,)),
            dma((groups,)),
            dma((groups, nz - 1)),
            dma((groups, nz - 1)),
            dma((experts,)),
            dma((experts,)),
        ],
        compiler_params=pltpu.CompilerParams(
            collective_id=0, has_side_effects=True, vmem_limit_bytes=64200000
        ),
    )(tokens, cotangent, expert_ids.T, route_weights.T, w_gate[0], w_up[0], w_down[0])
    outs = pl.pallas_call(
        store_kernel,
        name="store_results",
        out_shape=tuple(jax.ShapeDtypeStruct(shape, bf16) for shape in shapes),
        in_specs=[any_spec] * 5,
        out_specs=(any_spec,) * 5,
        scratch_shapes=[dma((5,))],
        compiler_params=pltpu.CompilerParams(vmem_limit_bytes=4 * 1024 * 1024),
    )(*outs)
    grad_tokens, grad_route, grad_gate, grad_up, grad_down = outs
    return grad_tokens, grad_route.T, grad_gate[None], grad_up[None], grad_down[None]


def body(tokens, cotangent, expert_ids, route_weights, w_gate, w_up, w_down):
    tok_count, topk = expert_ids.shape
    experts = lax.axis_size("ep")
    whole = 2 * tok_count * topk // experts >= tok_count
    paired = lax.axis_size("dp") == 4 and experts in (4, 8, 16) and tok_count in (16, 32, 64, 128)
    chosen = fused_body if whole and paired else routed_body
    return chosen(tokens, cotangent, expert_ids, route_weights, w_gate, w_up, w_down)


def solution(mesh):
    return jax.shard_map(
        body,
        mesh=mesh,
        in_specs=(
            P(("ep", "dp"), None),
            P(("ep", "dp"), None),
            P(("ep", "dp"), None),
            P(("ep", "dp"), None),
            P("ep", None, None),
            P("ep", None, None),
            P("ep", None, None),
        ),
        out_specs=(
            P(("ep", "dp"), None),
            P(("ep", "dp"), None),
            P("ep", "dp", None),
            P("ep", "dp", None),
            P("ep", None, "dp"),
        ),
        check_vma=False,
    )
```

```python
import jax
import jax.numpy as jnp
from jax import lax
from jax.experimental import pallas as pl
from jax.experimental.pallas import tpu as pltpu
from jax.sharding import PartitionSpec as P

block_rows = 128
contract_last = (((1,), (1,)), ((), ()))
contract_first = (((0,), (0,)), ((), ()))


def silu_parts(gate_pre):
    sig = jax.nn.sigmoid(gate_pre)
    return (gate_pre * sig, sig * (1.0 + gate_pre * (1.0 - sig)))


def expert_pass(rows_x, rows_cot, rows_w, live_count, w_gate_one, w_up_one, w_down_one):
    total, model = rows_x.shape
    width = w_gate_one.shape[1]

    def step(index, carry):
        acc_gate, acc_up, acc_down, slot_grad, route_grad = carry
        start = index * block_rows
        tok = lax.dynamic_slice_in_dim(rows_x, start, block_rows, 0)
        cot = lax.dynamic_slice_in_dim(rows_cot, start, block_rows, 0)
        weight = lax.dynamic_slice_in_dim(rows_w, start, block_rows, 0).astype(jnp.float32)[:, None]
        gate_pre = jnp.dot(tok, w_gate_one, preferred_element_type=jnp.float32)
        up_pre = jnp.dot(tok, w_up_one, preferred_element_type=jnp.float32)
        act, slope = silu_parts(gate_pre)
        hidden = lax.optimization_barrier((act * up_pre).astype(jnp.bfloat16))
        back = lax.dot_general(cot, w_down_one, contract_last, preferred_element_type=jnp.float32)
        route_part = jnp.sum(hidden.astype(jnp.float32) * back, axis=1)
        scaled = weight * back
        grad_gate_pre = (scaled * up_pre * slope).astype(jnp.bfloat16)
        grad_up_pre = (scaled * act).astype(jnp.bfloat16)
        scaled_cot = (weight * cot.astype(jnp.float32)).astype(jnp.bfloat16)
        part = lax.dot_general(
            grad_gate_pre, w_gate_one, contract_last, preferred_element_type=jnp.float32
        )
        part = part + lax.dot_general(
            grad_up_pre, w_up_one, contract_last, preferred_element_type=jnp.float32
        )
        acc_gate = acc_gate + lax.dot_general(
            tok, grad_gate_pre, contract_first, preferred_element_type=jnp.float32
        )
        acc_up = acc_up + lax.dot_general(
            tok, grad_up_pre, contract_first, preferred_element_type=jnp.float32
        )
        acc_down = acc_down + lax.dot_general(
            hidden, scaled_cot, contract_first, preferred_element_type=jnp.float32
        )
        slot_grad = lax.dynamic_update_slice_in_dim(slot_grad, part, start, 0)
        route_grad = lax.dynamic_update_slice_in_dim(route_grad, route_part, start, 0)
        return (acc_gate, acc_up, acc_down, slot_grad, route_grad)

    init = (
        jnp.zeros((model, width), jnp.float32),
        jnp.zeros((model, width), jnp.float32),
        jnp.zeros((width, model), jnp.float32),
        jnp.zeros((total, model), jnp.float32),
        jnp.zeros((total,), jnp.float32),
    )
    block_count = (live_count + block_rows - 1) // block_rows
    return lax.fori_loop(0, block_count, step, init)


def routed_body(tokens, cotangent, expert_ids, route_weights, w_gate, w_up, w_down):
    tok_count, topk = expert_ids.shape
    model = tokens.shape[1]
    experts = lax.axis_size("ep")
    capacity = min(tok_count, 2 * tok_count * topk // experts)
    slots = tok_count * topk
    row_total = experts * capacity
    flat_ids = expert_ids.reshape(slots)
    onehot = (flat_ids[:, None] == jnp.arange(experts, dtype=jnp.int32)[None, :]).astype(jnp.int32)
    position = jnp.sum((jnp.cumsum(onehot, axis=0) - 1) * onehot, axis=1)
    slot_ids = jnp.arange(slots, dtype=jnp.int32)
    source = (
        jnp.full((row_total,), slots, jnp.int32).at[flat_ids * capacity + position].set(slot_ids)
    )
    filled = source < slots
    source_token = jnp.where(filled, source // topk, tok_count)
    joined = jnp.concatenate([tokens, cotangent], axis=1)
    picked = jnp.take(joined, source_token, axis=0, mode="fill", fill_value=0)
    send_x = picked[:, :model].reshape(experts, capacity, model)
    send_cot = picked[:, model:].reshape(experts, capacity, model)
    send_w = jnp.take(
        route_weights.reshape(slots), jnp.where(filled, source, slots), mode="fill", fill_value=0
    ).reshape(experts, capacity)
    recv_x, recv_cot, recv_w = (
        lax.all_to_all(send_x, "ep", split_axis=0, concat_axis=0, tiled=True),
        lax.all_to_all(send_cot, "ep", split_axis=0, concat_axis=0, tiled=True),
        lax.all_to_all(send_w, "ep", split_axis=0, concat_axis=0, tiled=True),
    )
    flat_w = recv_w.reshape(row_total)
    live = (flat_w != 0).astype(jnp.int32)
    live_count = jnp.sum(live)
    place = jnp.where(live > 0, jnp.cumsum(live) - 1, row_total)
    anchor = (
        jnp.full((row_total,), row_total, jnp.int32)
        .at[place]
        .set(jnp.arange(row_total, dtype=jnp.int32), mode="drop")
    )
    recv_joined = jnp.concatenate(
        [recv_x.reshape(row_total, model), recv_cot.reshape(row_total, model)], axis=1
    )
    packed = jnp.take(recv_joined, anchor, axis=0, mode="fill", fill_value=0)
    pack_x = packed[:, :model]
    pack_cot = packed[:, model:]
    pack_w = jnp.take(flat_w, anchor, mode="fill", fill_value=0)
    w_gate_one = w_gate[0]
    w_up_one = w_up[0]
    w_down_one = w_down[0]
    acc_gate, acc_up, acc_down, slot_grad, route_grad = expert_pass(
        pack_x, pack_cot, pack_w, live_count, w_gate_one, w_up_one, w_down_one
    )
    slot_rows = jnp.take(slot_grad, place, axis=0, mode="fill", fill_value=0.0).astype(jnp.bfloat16)
    route_rows = jnp.take(route_grad, place, axis=0, mode="fill", fill_value=0.0).astype(
        jnp.bfloat16
    )
    back_x, back_route_rows = (
        lax.all_to_all(
            slot_rows.reshape(experts, capacity, model),
            "ep",
            split_axis=0,
            concat_axis=0,
            tiled=True,
        ),
        lax.all_to_all(
            route_rows.reshape(experts, capacity), "ep", split_axis=0, concat_axis=0, tiled=True
        ),
    )
    mine_rows = back_x[flat_ids, position].reshape(tok_count, topk, model)
    grad_tokens = jnp.sum(mine_rows.astype(jnp.float32), axis=1).astype(jnp.bfloat16)
    grad_route = back_route_rows[flat_ids, position].reshape(tok_count, topk)
    summed = (
        lax.psum_scatter(
            acc_gate[None].astype(jnp.bfloat16), "dp", scatter_dimension=1, tiled=True
        ).astype(jnp.float32),
        lax.psum_scatter(
            acc_up[None].astype(jnp.bfloat16), "dp", scatter_dimension=1, tiled=True
        ).astype(jnp.float32),
        lax.psum_scatter(
            acc_down[None].astype(jnp.bfloat16), "dp", scatter_dimension=2, tiled=True
        ).astype(jnp.float32),
    )
    return (
        grad_tokens,
        grad_route,
        summed[0].astype(jnp.bfloat16),
        summed[1].astype(jnp.bfloat16),
        summed[2].astype(jnp.bfloat16),
    )


def fused_kernel(
    tok_hbm, cot_hbm, ids_hbm, rw_hbm, wg_hbm, wu_hbm, wdn_hbm,
    gt_ref, route_ref, gg_ref, gu_ref, gd_ref,
    ids_ref, rw_ref, wg, wu, wdn, tc, wd, wbuf, cols, colst, act_buf, fac_buf, hid_buf, hw_own, hw_recv, gp_own, gp_recv,
    part, ys, yr, zs, zr, rs, rr, weight_buf, route_buf,
    l_sem, w_send, w_recv, g_send, g_recv, c_send, c_recv,
    h_send, h_done, y_send, y_recv, z_send, z_recv, r_send, r_recv,
):
    ep_size = lax.axis_size("ep")
    groups = lax.axis_size("dp")
    count = tok_hbm.shape[0]
    col = tc.shape[3]
    tiles, rows, ft = hw_own.shape
    nz = ep_size // 2
    half = rows // 2
    ep = lax.axis_index("ep")
    dp = lax.axis_index("dp")
    z, y = ep // 2, ep % 2
    xx, core = dp // 2, dp % 2
    mine = y * nz + z
    ynb = z * 2 + 1 - y
    peers_dp = (xx * 2 + 1 - core, (1 - xx) * 2 + core, (1 - xx) * 2 + 1 - core)
    f32 = jnp.float32
    bf16 = jnp.bfloat16

    def span(index, size):
        return pl.ds(pl.multiple_of(index * size, size), size)

    def remote(src, dst, send, recv, ep_to, dp_to):
        return pltpu.make_async_remote_copy(
            src_ref=src, dst_ref=dst, send_sem=send, recv_sem=recv,
            device_id=(ep_to, dp_to), device_id_type=pl.DeviceIdType.MESH,
        )

    loads = [
        pltpu.make_async_copy(ref.at[:, pl.ds(j * col, col)], tc.at[k, j, span(mine, count)], l_sem.at[k, j])
        for k, ref in enumerate((tok_hbm, cot_hbm))
        for j in range(groups)
    ]
    for load in loads:
        load.start()
    lists = (
        pltpu.make_async_copy(ids_hbm, ids_ref, l_sem.at[3, 0]),
        pltpu.make_async_copy(rw_hbm, rw_ref, l_sem.at[3, 1]),
    )
    for load in lists:
        load.start()
    w_loads = [
        pltpu.make_async_copy(src, dst, l_sem.at[2, 1 + k])
        for k, (src, dst) in enumerate(((wg_hbm, wg), (wu_hbm, wu), (wdn_hbm, wdn)))
    ]

    barrier = pltpu.get_barrier_semaphore()
    for k in range(1, ep_size):
        pl.semaphore_signal(
            barrier, inc=1, device_id=((ep + k) % ep_size, dp), device_id_type=pl.DeviceIdType.MESH
        )
    for peer in peers_dp:
        pl.semaphore_signal(barrier, inc=1, device_id=(ep, peer), device_id_type=pl.DeviceIdType.MESH)
    wd[...] = jnp.zeros(wd.shape, f32)
    rs[...] = jnp.zeros(rs.shape, f32)
    for load in lists:
        load.wait()
    ids = ids_ref[...]
    values = rw_ref[...].astype(f32)
    for e in range(ep_size):
        line = jnp.sum(jnp.where(ids == e, values, 0.0), axis=0, keepdims=True)
        wd[e, :, 0:count] = jnp.broadcast_to(line, (wd.shape[1], count))
    pl.semaphore_wait(barrier, ep_size - 1 + len(peers_dp))

    def block(which, zz, yy):
        if which == 2:
            return cols.at[1, pl.ds(1, 2), span(yy * nz + zz, count)]
        return tc.at[which, :, span(yy * nz + zz, count)]

    def block_copy(which, way, zz, ep_to):
        view = block(which, zz, y)
        return remote(view, view, g_send.at[which, way, zz], g_recv.at[which, y * nz + zz], ep_to, dp)

    def send_up(which, zz):
        @pl.when(z + 1 < nz)
        def _():
            block_copy(which, 0, zz, ep + 2).start()

    def send_down(which, zz):
        @pl.when(z > 0)
        def _():
            block_copy(which, 1, zz, ep - 2).start()

    def send_side(which, zz):
        block_copy(which, 2, zz, ynb).start()

    def send_cols(which, pos, reach=3):
        if which == 2:
            return
        for r, peer in enumerate(peers_dp[:reach]):
            remote(
                tc.at[which, peer, span(pos, count)],
                cols.at[which, r, span(pos, count)],
                c_send.at[which, r], c_recv.at[which, r], ep, peer,
            ).start()

    def pass_on(which, d):
        @pl.when(z >= d)
        def _():
            block_copy(which, 0, z - d, ep).wait_recv()
            send_up(which, z - d)
            send_side(which, z - d)
            send_cols(which, y * nz + z - d, 3 - 2 * which)

        @pl.when(z + d < nz)
        def _():
            block_copy(which, 1, z + d, ep).wait_recv()
            send_down(which, z + d)
            send_side(which, z + d)
            send_cols(which, y * nz + z + d, 3 - 2 * which)

    def take_side(which):
        def take(k, carry):
            zz = (z + k) % nz
            pos = (1 - y) * nz + zz
            view = block(which, zz, 1 - y)
            remote(view, view, g_send.at[which, 2, zz], g_recv.at[which, pos], ep, dp).wait_recv()
            send_cols(which, pos, 3 - 2 * which)
            return carry

        lax.fori_loop(0, nz, take, 0)

    def h_copy(kind, r, t, forwarded=False):
        if kind == 0:
            src = hw_recv.at[1, t] if forwarded else hw_own.at[t]
            dst = hw_recv.at[r, t]
        else:
            sub = span(y if kind == 1 else 1 - y, half)
            src = gp_recv.at[1, t, :, sub] if forwarded else gp_own.at[t, :, sub]
            dst = gp_recv.at[r, t, :, sub]
        peer = peers_dp[0] if forwarded else peers_dp[r]
        return remote(src, dst, h_send.at[kind, r, t], h_done.at[kind, r, t], ep, peer)

    def forward(kind, t):
        h_copy(kind, 1, t).wait_recv()
        h_copy(kind, 2, t, True).start()

    for which in range(2):
        for load in loads[which * groups:(which + 1) * groups]:
            load.wait()
        send_up(which, z)
        send_down(which, z)
        send_side(which, z)
        send_cols(which, mine)
    wbuf[mine] = wd[ep]
    for k in range(1, ep_size):
        to = (ep + k) % ep_size
        remote(wd.at[to], wbuf.at[mine], w_send.at[k], w_recv.at[mine], to, dp).start()
    for load in w_loads:
        load.start()
    for d in range(1, nz):
        pass_on(0, d)
    take_side(0)
    for k in range(1, ep_size):
        frm = (ep + k) % ep_size
        pos = (frm % 2) * nz + frm // 2
        remote(wd.at[frm], wbuf.at[pos], w_send.at[k], w_recv.at[pos], ep, dp).wait_recv()
    for load in w_loads:
        load.wait()
    flat = wbuf[...].reshape(ep_size * wbuf.shape[1], wbuf.shape[2])
    turned = jnp.concatenate([flat] * (128 // flat.shape[0]), axis=0).T
    step = wbuf.shape[1]
    weight = jnp.concatenate([turned[0:count, p * step:p * step + 1] for p in range(ep_size)], axis=0)
    weight_buf[...] = jnp.broadcast_to(weight, weight_buf.shape)

    for t in range(max(tiles, nz - 1)):
        if t < nz - 1:
            pass_on(1, t + 1)
        if t < tiles:
            lanes = pl.ds(t * ft, ft)
            gate_pre = jnp.zeros((rows, ft), f32)
            up_pre = jnp.zeros((rows, ft), f32)
            for j in range(groups):
                depth = pl.ds(j * col, col)
                gate_pre += jnp.dot(tc[0, j], wg[depth, lanes], preferred_element_type=f32)
                up_pre += jnp.dot(tc[0, j], wu[depth, lanes], preferred_element_type=f32)
            act, slope = silu_parts(gate_pre)
            product = act * up_pre
            hw_own[t] = (weight * product).astype(bf16)
            act_buf[t] = act
            fac_buf[t] = up_pre * slope
            hid_buf[t] = product.astype(bf16)
            for r in (1, 0):
                h_copy(0, r, t).start()
    def back_rows(kind):
        sub = span(y if kind == 1 else 1 - y, half)
        factor = weight_buf[sub, 0:1]

        def back_step(t, route):
            back = jnp.zeros((half, ft), f32)
            for j in range(groups):
                back += lax.dot_general(
                    tc[1, j, sub, :], wdn[span(t, ft), pl.ds(j * col, col)], contract_last, preferred_element_type=f32
                )
            scaled = factor * back
            gp_own[t, 0, sub, :] = (scaled * fac_buf[t, sub, :]).astype(bf16)
            gp_own[t, 1, sub, :] = (scaled * act_buf[t, sub, :]).astype(bf16)
            route = route + jnp.sum(hid_buf[t, sub, :].astype(f32) * back, axis=1, keepdims=True)
            for r in (1, 0):
                h_copy(kind, r, t).start()
            return route

        route = lax.fori_loop(0, tiles, back_step, jnp.zeros((half, 1), f32))
        route_buf[sub, :] = jnp.broadcast_to(route, (half, route_buf.shape[1]))

    back_rows(1)
    for r in (1, 2):
        view = cols.at[1, r, span(mine, count)]
        remote(view, view, c_send.at[1, r], c_recv.at[1, r], ep, peers_dp[r]).wait_recv()
    send_up(2, z)
    send_down(2, z)
    take_side(1)
    send_side(2, z)
    pass_on(2, 1)

    back_rows(2)
    for d in range(2, nz):
        pass_on(2, d)
    lined = route_buf[...].T
    for p in range(ep_size):
        line = lined[0:1, p * count:(p + 1) * count]
        rs[p, :, 0:count] = jnp.broadcast_to(line, (rs.shape[1], count))

    def slot_step(n, carry):
        total = jnp.zeros((rows, col), f32)
        for t in range(tiles):
            lanes = pl.ds(t * ft, ft)
            total += lax.dot_general(gp_own[t, 0], wg[span(n, col), lanes], contract_last, preferred_element_type=f32)
            total += lax.dot_general(gp_own[t, 1], wu[span(n, col), lanes], contract_last, preferred_element_type=f32)
        part[n] = total.reshape(2, half, col)
        ys[n] = part[n, 1 - y].astype(bf16)
        remote(ys.at[n], yr.at[n], y_send.at[n], y_recv.at[n], ynb, dp).start()
        return carry

    lax.fori_loop(0, groups, slot_step, 0)
    for k in range(1, ep_size):
        to = (ep + k) % ep_size
        pos = (to % 2) * nz + to // 2
        remote(rs.at[pos], rr.at[ep], r_send.at[k], r_recv.at[ep], to, dp).start()
    rr[ep] = rs[mine]
    for t in range(tiles):
        forward(0, t)

    def add_step(n, carry):
        remote(ys.at[n], yr.at[n], y_send.at[n], y_recv.at[n], ynb, dp).wait()
        total = part[n, y] + yr[n].astype(f32)
        part[n, y] = total
        zs[n] = total.astype(bf16)
        for k in range(1, nz):
            to = (z + k) % nz
            remote(
                zs.at[n, span(to, count)], zr.at[n, k - 1], z_send.at[n, k - 1], z_recv.at[n, k - 1], to * 2 + y, dp
            ).start()
        return carry

    lax.fori_loop(0, groups, add_step, 0)
    colst[0] = tc[0, dp].T
    for r in range(3):
        remote(cols.at[0, r], cols.at[0, r], c_send.at[0, r], c_recv.at[0, r], ep, peers_dp[r]).wait_recv()
        colst[1 + r] = cols[0, r].T
    remote(cols.at[1, 0], cols.at[1, 0], c_send.at[1, 0], c_recv.at[1, 0], ep, peers_dp[0]).wait_recv()
    take_side(2)
    for t in range(tiles):
        forward(1, t)
    forward(2, 0)

    def down_step(t, carry):
        for r in (0, 2):
            h_copy(0, r, t).wait_recv()
        blocks = [hw_own.at[t]] + [hw_recv.at[r, t] for r in range(3)]
        cots = [tc.at[1, dp]] + [cols.at[1, r] for r in range(3)]
        grad_down = jnp.zeros((ft, col), f32)
        for g in range(4):
            grad_down += lax.dot_general(blocks[g][...], cots[g][...], contract_first, preferred_element_type=f32)
        gd_ref[span(t, ft), :] = grad_down.astype(bf16)
        return carry

    lax.fori_loop(0, tiles, down_step, 0)

    def sum_step(n, carry):
        total = part[n, y, span(z, count), :]
        for k in range(1, nz):
            remote(
                zs.at[n, pl.ds(0, count)], zr.at[n, k - 1], z_send.at[n, k - 1], z_recv.at[n, k - 1], ep, dp
            ).wait()
            total = total + zr[n, k - 1].astype(f32)
        gt_ref[:, span(n, col)] = total.astype(bf16)
        return carry

    def weight_step(t, carry):
        @pl.when(t + 1 < tiles)
        def _():
            forward(2, t + 1)

        @pl.when(t + 1 == tiles)
        def _():
            lax.fori_loop(0, groups, sum_step, 0)

        for kind in (1, 2):
            for r in (0, 2):
                h_copy(kind, r, t).wait_recv()
        blocks = [gp_own.at[t]] + [gp_recv.at[r, t] for r in range(3)]
        grad_gate = jnp.zeros((col, ft), f32)
        grad_up = jnp.zeros((col, ft), f32)
        for g in range(4):
            grad_gate += jnp.dot(colst[g], blocks[g][0], preferred_element_type=f32)
            grad_up += jnp.dot(colst[g], blocks[g][1], preferred_element_type=f32)
        gg_ref[:, span(t, ft)] = grad_gate.astype(bf16)
        gu_ref[:, span(t, ft)] = grad_up.astype(bf16)
        return carry

    lax.fori_loop(0, tiles, weight_step, 0)

    for k in range(1, ep_size):
        frm = (ep + k) % ep_size
        remote(rs.at[0], rr.at[frm], r_send.at[k], r_recv.at[frm], ep, dp).wait()
        remote(wd.at[0], wbuf.at[mine], w_send.at[k], w_recv.at[mine], ep, dp).wait_send()
    table = jnp.zeros(ids.shape, f32)
    for e in range(ep_size):
        table = table + jnp.where(ids == e, rr[e, 0:1, 0:count], 0.0)
    route_ref[...] = table.astype(bf16)
    for which in range(3):
        for zz in range(nz):
            block_copy(which, 2, zz, ep).wait_send()

            @pl.when(jnp.logical_and(z >= zz, z + 1 < nz))
            def _():
                block_copy(which, 0, zz, ep).wait_send()

            @pl.when(jnp.logical_and(z <= zz, z > 0))
            def _():
                block_copy(which, 1, zz, ep).wait_send()

    for which in range(2):
        for r in range(3):
            view = cols.at[1, r, span(mine, count)] if which == 1 and r > 0 else cols.at[which, r]
            remote(view, view, c_send.at[which, r], c_recv.at[which, r], ep, peers_dp[r]).wait_send()
    for kind in range(3):
        for t in range(tiles):
            for r in range(3):
                h_copy(kind, r, t).wait_send()


def store_kernel(*refs):
    sems = refs[-1]
    each = (len(refs) - 1) // 2
    copies = [pltpu.make_async_copy(refs[k], refs[each + k], sems.at[k]) for k in range(each)]
    for copy in copies:
        copy.start()
    for copy in copies:
        copy.wait()


def fused_body(tokens, cotangent, expert_ids, route_weights, w_gate, w_up, w_down):
    count, topk = expert_ids.shape
    model = tokens.shape[1]
    experts = lax.axis_size("ep")
    groups = lax.axis_size("dp")
    width = w_gate.shape[2]
    rows = experts * count
    col = model // groups
    ft = 256 if width % 256 == 0 else width
    tiles = width // ft
    lanes = 128
    bf16 = jnp.bfloat16
    f32 = jnp.float32
    any_spec = pl.BlockSpec(memory_space=pl.ANY)
    hbm = pl.BlockSpec(memory_space=pltpu.HBM)
    vmem = pl.BlockSpec(memory_space=pltpu.VMEM)
    dma = pltpu.SemaphoreType.DMA
    nz = experts // 2
    small = (experts, 8, lanes)
    shapes = ((count, model), (topk, count), (col, width), (col, width), (width, col))
    outs = pl.pallas_call(
        fused_kernel,
        name="fused_layer",
        out_shape=tuple(pltpu.VMEM(shape, bf16) for shape in shapes),
        in_specs=[hbm] * 7,
        out_specs=(vmem,) * 5,
        scratch_shapes=[
            pltpu.VMEM((topk, count), jnp.int32),
            pltpu.VMEM((topk, count), bf16),
            pltpu.VMEM((model, width), bf16),
            pltpu.VMEM((model, width), bf16),
            pltpu.VMEM((width, model), bf16),
            pltpu.VMEM((2, groups, rows, col), bf16),
            pltpu.VMEM(small, f32),
            pltpu.VMEM(small, f32),
            pltpu.VMEM((2, 3, rows, col), bf16),
            pltpu.VMEM((4, col, rows), bf16),
            pltpu.VMEM((tiles, rows, ft), f32),
            pltpu.VMEM((tiles, rows, ft), f32),
            pltpu.VMEM((tiles, rows, ft), bf16),
            pltpu.VMEM((tiles, rows, ft), bf16),
            pltpu.VMEM((3, tiles, rows, ft), bf16),
            pltpu.VMEM((tiles, 2, rows, ft), bf16),
            pltpu.VMEM((3, tiles, 2, rows, ft), bf16),
            pltpu.VMEM((groups, 2, rows // 2, col), f32),
            pltpu.VMEM((groups, rows // 2, col), bf16),
            pltpu.VMEM((groups, rows // 2, col), bf16),
            pltpu.VMEM((groups, rows // 2, col), bf16),
            pltpu.VMEM((groups, nz - 1, count, col), bf16),
            pltpu.VMEM(small, f32),
            pltpu.VMEM(small, f32),
            pltpu.VMEM((rows, lanes), f32),
            pltpu.VMEM((rows, lanes), f32),
            dma((4, max(groups, 4))),
            dma((experts,)),
            dma((experts,)),
            dma((3, 3, nz)),
            dma((3, experts)),
            dma((2, 3)),
            dma((2, 3)),
            dma((3, 3, tiles)),
            dma((3, 3, tiles)),
            dma((groups,)),
            dma((groups,)),
            dma((groups, nz - 1)),
            dma((groups, nz - 1)),
            dma((experts,)),
            dma((experts,)),
        ],
        compiler_params=pltpu.CompilerParams(
            collective_id=0, has_side_effects=True, vmem_limit_bytes=64200000
        ),
    )(tokens, cotangent, expert_ids.T, route_weights.T, w_gate[0], w_up[0], w_down[0])
    outs = pl.pallas_call(
        store_kernel,
        name="store_results",
        out_shape=tuple(jax.ShapeDtypeStruct(shape, bf16) for shape in shapes),
        in_specs=[any_spec] * 5,
        out_specs=(any_spec,) * 5,
        scratch_shapes=[dma((5,))],
        compiler_params=pltpu.CompilerParams(vmem_limit_bytes=4 * 1024 * 1024),
    )(*outs)
    grad_tokens, grad_route, grad_gate, grad_up, grad_down = outs
    return grad_tokens, grad_route.T, grad_gate[None], grad_up[None], grad_down[None]


def body(tokens, cotangent, expert_ids, route_weights, w_gate, w_up, w_down):
    tok_count, topk = expert_ids.shape
    experts = lax.axis_size("ep")
    whole = 2 * tok_count * topk // experts >= tok_count
    paired = lax.axis_size("dp") == 4 and experts in (4, 8, 16) and tok_count in (16, 32, 64, 128)
    chosen = fused_body if whole and paired else routed_body
    return chosen(tokens, cotangent, expert_ids, route_weights, w_gate, w_up, w_down)


def solution(mesh):
    return jax.shard_map(
        body,
        mesh=mesh,
        in_specs=(
            P(("ep", "dp"), None),
            P(("ep", "dp"), None),
            P(("ep", "dp"), None),
            P(("ep", "dp"), None),
            P("ep", None, None),
            P("ep", None, None),
            P("ep", None, None),
        ),
        out_specs=(
            P(("ep", "dp"), None),
            P(("ep", "dp"), None),
            P("ep", "dp", None),
            P("ep", "dp", None),
            P("ep", None, "dp"),
        ),
        check_vma=False,
    )
```

```python
import jax
import jax.numpy as jnp
from jax import lax
from jax.experimental import pallas as pl
from jax.experimental.pallas import tpu as pltpu
from jax.sharding import PartitionSpec as P

block_rows = 128
contract_last = (((1,), (1,)), ((), ()))
contract_first = (((0,), (0,)), ((), ()))


def silu_parts(gate_pre):
    sig = jax.nn.sigmoid(gate_pre)
    return (gate_pre * sig, sig * (1.0 + gate_pre * (1.0 - sig)))


def expert_pass(rows_x, rows_cot, rows_w, live_count, w_gate_one, w_up_one, w_down_one):
    total, model = rows_x.shape
    width = w_gate_one.shape[1]

    def step(index, carry):
        acc_gate, acc_up, acc_down, slot_grad, route_grad = carry
        start = index * block_rows
        tok = lax.dynamic_slice_in_dim(rows_x, start, block_rows, 0)
        cot = lax.dynamic_slice_in_dim(rows_cot, start, block_rows, 0)
        weight = lax.dynamic_slice_in_dim(rows_w, start, block_rows, 0).astype(jnp.float32)[:, None]
        gate_pre = jnp.dot(tok, w_gate_one, preferred_element_type=jnp.float32)
        up_pre = jnp.dot(tok, w_up_one, preferred_element_type=jnp.float32)
        act, slope = silu_parts(gate_pre)
        hidden = lax.optimization_barrier((act * up_pre).astype(jnp.bfloat16))
        back = lax.dot_general(cot, w_down_one, contract_last, preferred_element_type=jnp.float32)
        route_part = jnp.sum(hidden.astype(jnp.float32) * back, axis=1)
        scaled = weight * back
        grad_gate_pre = (scaled * up_pre * slope).astype(jnp.bfloat16)
        grad_up_pre = (scaled * act).astype(jnp.bfloat16)
        scaled_cot = (weight * cot.astype(jnp.float32)).astype(jnp.bfloat16)
        part = lax.dot_general(
            grad_gate_pre, w_gate_one, contract_last, preferred_element_type=jnp.float32
        )
        part = part + lax.dot_general(
            grad_up_pre, w_up_one, contract_last, preferred_element_type=jnp.float32
        )
        acc_gate = acc_gate + lax.dot_general(
            tok, grad_gate_pre, contract_first, preferred_element_type=jnp.float32
        )
        acc_up = acc_up + lax.dot_general(
            tok, grad_up_pre, contract_first, preferred_element_type=jnp.float32
        )
        acc_down = acc_down + lax.dot_general(
            hidden, scaled_cot, contract_first, preferred_element_type=jnp.float32
        )
        slot_grad = lax.dynamic_update_slice_in_dim(slot_grad, part, start, 0)
        route_grad = lax.dynamic_update_slice_in_dim(route_grad, route_part, start, 0)
        return (acc_gate, acc_up, acc_down, slot_grad, route_grad)

    init = (
        jnp.zeros((model, width), jnp.float32),
        jnp.zeros((model, width), jnp.float32),
        jnp.zeros((width, model), jnp.float32),
        jnp.zeros((total, model), jnp.float32),
        jnp.zeros((total,), jnp.float32),
    )
    block_count = (live_count + block_rows - 1) // block_rows
    return lax.fori_loop(0, block_count, step, init)


def routed_body(tokens, cotangent, expert_ids, route_weights, w_gate, w_up, w_down):
    tok_count, topk = expert_ids.shape
    model = tokens.shape[1]
    experts = lax.axis_size("ep")
    capacity = min(tok_count, 2 * tok_count * topk // experts)
    slots = tok_count * topk
    row_total = experts * capacity
    flat_ids = expert_ids.reshape(slots)
    onehot = (flat_ids[:, None] == jnp.arange(experts, dtype=jnp.int32)[None, :]).astype(jnp.int32)
    position = jnp.sum((jnp.cumsum(onehot, axis=0) - 1) * onehot, axis=1)
    slot_ids = jnp.arange(slots, dtype=jnp.int32)
    source = (
        jnp.full((row_total,), slots, jnp.int32).at[flat_ids * capacity + position].set(slot_ids)
    )
    filled = source < slots
    source_token = jnp.where(filled, source // topk, tok_count)
    joined = jnp.concatenate([tokens, cotangent], axis=1)
    picked = jnp.take(joined, source_token, axis=0, mode="fill", fill_value=0)
    send_x = picked[:, :model].reshape(experts, capacity, model)
    send_cot = picked[:, model:].reshape(experts, capacity, model)
    send_w = jnp.take(
        route_weights.reshape(slots), jnp.where(filled, source, slots), mode="fill", fill_value=0
    ).reshape(experts, capacity)
    recv_x, recv_cot, recv_w = (
        lax.all_to_all(send_x, "ep", split_axis=0, concat_axis=0, tiled=True),
        lax.all_to_all(send_cot, "ep", split_axis=0, concat_axis=0, tiled=True),
        lax.all_to_all(send_w, "ep", split_axis=0, concat_axis=0, tiled=True),
    )
    flat_w = recv_w.reshape(row_total)
    live = (flat_w != 0).astype(jnp.int32)
    live_count = jnp.sum(live)
    place = jnp.where(live > 0, jnp.cumsum(live) - 1, row_total)
    anchor = (
        jnp.full((row_total,), row_total, jnp.int32)
        .at[place]
        .set(jnp.arange(row_total, dtype=jnp.int32), mode="drop")
    )
    recv_joined = jnp.concatenate(
        [recv_x.reshape(row_total, model), recv_cot.reshape(row_total, model)], axis=1
    )
    packed = jnp.take(recv_joined, anchor, axis=0, mode="fill", fill_value=0)
    pack_x = packed[:, :model]
    pack_cot = packed[:, model:]
    pack_w = jnp.take(flat_w, anchor, mode="fill", fill_value=0)
    w_gate_one = w_gate[0]
    w_up_one = w_up[0]
    w_down_one = w_down[0]
    acc_gate, acc_up, acc_down, slot_grad, route_grad = expert_pass(
        pack_x, pack_cot, pack_w, live_count, w_gate_one, w_up_one, w_down_one
    )
    slot_rows = jnp.take(slot_grad, place, axis=0, mode="fill", fill_value=0.0).astype(jnp.bfloat16)
    route_rows = jnp.take(route_grad, place, axis=0, mode="fill", fill_value=0.0).astype(
        jnp.bfloat16
    )
    back_x, back_route_rows = (
        lax.all_to_all(
            slot_rows.reshape(experts, capacity, model),
            "ep",
            split_axis=0,
            concat_axis=0,
            tiled=True,
        ),
        lax.all_to_all(
            route_rows.reshape(experts, capacity), "ep", split_axis=0, concat_axis=0, tiled=True
        ),
    )
    mine_rows = back_x[flat_ids, position].reshape(tok_count, topk, model)
    grad_tokens = jnp.sum(mine_rows.astype(jnp.float32), axis=1).astype(jnp.bfloat16)
    grad_route = back_route_rows[flat_ids, position].reshape(tok_count, topk)
    summed = (
        lax.psum_scatter(
            acc_gate[None].astype(jnp.bfloat16), "dp", scatter_dimension=1, tiled=True
        ).astype(jnp.float32),
        lax.psum_scatter(
            acc_up[None].astype(jnp.bfloat16), "dp", scatter_dimension=1, tiled=True
        ).astype(jnp.float32),
        lax.psum_scatter(
            acc_down[None].astype(jnp.bfloat16), "dp", scatter_dimension=2, tiled=True
        ).astype(jnp.float32),
    )
    return (
        grad_tokens,
        grad_route,
        summed[0].astype(jnp.bfloat16),
        summed[1].astype(jnp.bfloat16),
        summed[2].astype(jnp.bfloat16),
    )


def fused_kernel(
    tok_hbm, cot_hbm, ids_hbm, rw_hbm, wg_hbm, wu_hbm, wdn_hbm,
    gt_ref, route_ref, gg_ref, gu_ref, gd_ref,
    ids_ref, rw_ref, wg, wu, wdn, tc, wd, wbuf, cols, colst, act_buf, fac_buf, hid_buf, hw_own, hw_recv, gp_own, gp_recv,
    part, ys, yr, zs, zr, rs, rr, weight_buf, route_buf,
    l_sem, w_send, w_recv, g_send, g_recv, c_send, c_recv,
    h_send, h_done, y_send, y_recv, z_send, z_recv, r_send, r_recv,
):
    ep_size = lax.axis_size("ep")
    groups = lax.axis_size("dp")
    count = tok_hbm.shape[0]
    col = tc.shape[3]
    tiles, rows, ft = hw_own.shape
    nz = ep_size // 2
    half = rows // 2
    ep = lax.axis_index("ep")
    dp = lax.axis_index("dp")
    z, y = ep // 2, ep % 2
    xx, core = dp // 2, dp % 2
    mine = y * nz + z
    ynb = z * 2 + 1 - y
    peers_dp = (xx * 2 + 1 - core, (1 - xx) * 2 + core, (1 - xx) * 2 + 1 - core)
    f32 = jnp.float32
    bf16 = jnp.bfloat16

    def span(index, size):
        return pl.ds(pl.multiple_of(index * size, size), size)

    def remote(src, dst, send, recv, ep_to, dp_to):
        return pltpu.make_async_remote_copy(
            src_ref=src, dst_ref=dst, send_sem=send, recv_sem=recv,
            device_id=(ep_to, dp_to), device_id_type=pl.DeviceIdType.MESH,
        )

    loads = [
        pltpu.make_async_copy(ref.at[:, pl.ds(j * col, col)], tc.at[k, j, span(mine, count)], l_sem.at[k, j])
        for k, ref in enumerate((tok_hbm, cot_hbm))
        for j in range(groups)
    ]
    for load in loads:
        load.start()
    lists = (
        pltpu.make_async_copy(ids_hbm, ids_ref, l_sem.at[3, 0]),
        pltpu.make_async_copy(rw_hbm, rw_ref, l_sem.at[3, 1]),
    )
    for load in lists:
        load.start()
    w_loads = [
        pltpu.make_async_copy(src, dst, l_sem.at[2, 1 + k])
        for k, (src, dst) in enumerate(((wg_hbm, wg), (wu_hbm, wu), (wdn_hbm, wdn)))
    ]

    barrier = pltpu.get_barrier_semaphore()
    for k in range(1, ep_size):
        pl.semaphore_signal(
            barrier, inc=1, device_id=((ep + k) % ep_size, dp), device_id_type=pl.DeviceIdType.MESH
        )
    for peer in peers_dp:
        pl.semaphore_signal(barrier, inc=1, device_id=(ep, peer), device_id_type=pl.DeviceIdType.MESH)
    wd[...] = jnp.zeros(wd.shape, f32)
    rs[...] = jnp.zeros(rs.shape, f32)
    for load in lists:
        load.wait()
    ids = ids_ref[...]
    values = rw_ref[...].astype(f32)
    for e in range(ep_size):
        line = jnp.sum(jnp.where(ids == e, values, 0.0), axis=0, keepdims=True)
        wd[e, :, 0:count] = jnp.broadcast_to(line, (wd.shape[1], count))
    pl.semaphore_wait(barrier, ep_size - 1 + len(peers_dp))

    def block(which, zz, yy):
        if which == 2:
            return cols.at[1, pl.ds(1, 2), span(yy * nz + zz, count)]
        return tc.at[which, :, span(yy * nz + zz, count)]

    def block_copy(which, way, zz, ep_to):
        view = block(which, zz, y)
        return remote(view, view, g_send.at[which, way, zz], g_recv.at[which, y * nz + zz], ep_to, dp)

    def send_up(which, zz):
        @pl.when(z + 1 < nz)
        def _():
            block_copy(which, 0, zz, ep + 2).start()

    def send_down(which, zz):
        @pl.when(z > 0)
        def _():
            block_copy(which, 1, zz, ep - 2).start()

    def send_side(which, zz):
        block_copy(which, 2, zz, ynb).start()

    def send_cols(which, pos, reach=3, side=False):
        if which == 2:
            return
        for r, peer in enumerate(peers_dp[:reach]):
            remote(
                tc.at[which, peer, span(pos, count)],
                cols.at[which, r, span(pos, count)],
                c_send.at[2 if side and r > 0 else which, r], c_recv.at[2 if side and r > 0 else which, r], ep, peer,
            ).start()

    def pass_on(which, d):
        @pl.when(z >= d)
        def _():
            block_copy(which, 0, z - d, ep).wait_recv()
            send_up(which, z - d)
            if which < 2:
                send_side(which, z - d)
            send_cols(which, y * nz + z - d, 3 - 2 * which)

        @pl.when(z + d < nz)
        def _():
            block_copy(which, 1, z + d, ep).wait_recv()
            send_down(which, z + d)
            if which < 2:
                send_side(which, z + d)
            send_cols(which, y * nz + z + d, 3 - 2 * which)

    def take_side(which):
        def take(k, carry):
            zz = (z + k) % nz
            pos = (1 - y) * nz + zz
            view = block(which, zz, 1 - y)
            remote(view, view, g_send.at[which, 2, zz], g_recv.at[which, pos], ep, dp).wait_recv()
            send_cols(which, pos, 3, which == 1)
            return carry

        lax.fori_loop(0, nz, take, 0)

    def h_copy(kind, r, t, forwarded=False):
        if kind == 0:
            src = hw_recv.at[1, t] if forwarded else hw_own.at[t]
            dst = hw_recv.at[r, t]
        else:
            sub = span(y if kind == 1 else 1 - y, half)
            src = gp_recv.at[1, t, :, sub] if forwarded else gp_own.at[t, :, sub]
            dst = gp_recv.at[r, t, :, sub]
        peer = peers_dp[0] if forwarded else peers_dp[r]
        return remote(src, dst, h_send.at[kind, r, t], h_done.at[kind, r, t], ep, peer)

    def forward(kind, t):
        h_copy(kind, 1, t).wait_recv()
        h_copy(kind, 2, t, True).start()

    for which in range(2):
        for load in loads[which * groups:(which + 1) * groups]:
            load.wait()
        send_up(which, z)
        send_down(which, z)
        send_side(which, z)
        send_cols(which, mine)
    wbuf[mine] = wd[ep]
    for k in range(1, ep_size):
        to = (ep + k) % ep_size
        remote(wd.at[to], wbuf.at[mine], w_send.at[k], w_recv.at[mine], to, dp).start()
    for load in w_loads:
        load.start()
    for d in range(1, nz):
        pass_on(0, d)
    take_side(0)
    for k in range(1, ep_size):
        frm = (ep + k) % ep_size
        pos = (frm % 2) * nz + frm // 2
        remote(wd.at[frm], wbuf.at[pos], w_send.at[k], w_recv.at[pos], ep, dp).wait_recv()
    for load in w_loads:
        load.wait()
    flat = wbuf[...].reshape(ep_size * wbuf.shape[1], wbuf.shape[2])
    turned = jnp.concatenate([flat] * (128 // flat.shape[0]), axis=0).T
    step = wbuf.shape[1]
    weight = jnp.concatenate([turned[0:count, p * step:p * step + 1] for p in range(ep_size)], axis=0)
    weight_buf[...] = jnp.broadcast_to(weight, weight_buf.shape)

    for t in range(max(tiles, nz - 1)):
        if t < nz - 1:
            pass_on(1, t + 1)
        if t < tiles:
            lanes = pl.ds(t * ft, ft)
            gate_pre = jnp.zeros((rows, ft), f32)
            up_pre = jnp.zeros((rows, ft), f32)
            for j in range(groups):
                depth = pl.ds(j * col, col)
                gate_pre += jnp.dot(tc[0, j], wg[depth, lanes], preferred_element_type=f32)
                up_pre += jnp.dot(tc[0, j], wu[depth, lanes], preferred_element_type=f32)
            act, slope = silu_parts(gate_pre)
            product = act * up_pre
            hw_own[t] = (weight * product).astype(bf16)
            act_buf[t] = act
            fac_buf[t] = up_pre * slope
            hid_buf[t] = product.astype(bf16)
            for r in (1, 0):
                h_copy(0, r, t).start()
    def back_rows(kind):
        sub = span(y if kind == 1 else 1 - y, half)
        factor = weight_buf[sub, 0:1]

        def back_step(t, route):
            back = jnp.zeros((half, ft), f32)
            for j in range(groups):
                back += lax.dot_general(
                    tc[1, j, sub, :], wdn[span(t, ft), pl.ds(j * col, col)], contract_last, preferred_element_type=f32
                )
            scaled = factor * back
            gp_own[t, 0, sub, :] = (scaled * fac_buf[t, sub, :]).astype(bf16)
            gp_own[t, 1, sub, :] = (scaled * act_buf[t, sub, :]).astype(bf16)
            route = route + jnp.sum(hid_buf[t, sub, :].astype(f32) * back, axis=1, keepdims=True)
            for r in (1, 0):
                h_copy(kind, r, t).start()
            return route

        route = lax.fori_loop(0, tiles, back_step, jnp.zeros((half, 1), f32))
        route_buf[sub, :] = jnp.broadcast_to(route, (half, route_buf.shape[1]))

    back_rows(1)
    for r in (1, 2):
        view = cols.at[1, r, span(mine, count)]
        remote(view, view, c_send.at[1, r], c_recv.at[1, r], ep, peers_dp[r]).wait_recv()
    send_up(2, z)
    send_down(2, z)
    take_side(1)
    pass_on(2, 1)

    back_rows(2)
    for d in range(2, nz):
        pass_on(2, d)
    lined = route_buf[...].T
    for p in range(ep_size):
        line = lined[0:1, p * count:(p + 1) * count]
        rs[p, :, 0:count] = jnp.broadcast_to(line, (rs.shape[1], count))

    def slot_step(n, carry):
        total = jnp.zeros((rows, col), f32)
        for t in range(tiles):
            lanes = pl.ds(t * ft, ft)
            total += lax.dot_general(gp_own[t, 0], wg[span(n, col), lanes], contract_last, preferred_element_type=f32)
            total += lax.dot_general(gp_own[t, 1], wu[span(n, col), lanes], contract_last, preferred_element_type=f32)
        part[n] = total.reshape(2, half, col)
        ys[n] = part[n, 1 - y].astype(bf16)
        remote(ys.at[n], yr.at[n], y_send.at[n], y_recv.at[n], ynb, dp).start()
        return carry

    lax.fori_loop(0, groups, slot_step, 0)
    for k in range(1, ep_size):
        to = (ep + k) % ep_size
        pos = (to % 2) * nz + to // 2
        remote(rs.at[pos], rr.at[ep], r_send.at[k], r_recv.at[ep], to, dp).start()
    rr[ep] = rs[mine]
    for t in range(tiles):
        forward(0, t)

    def add_step(n, carry):
        remote(ys.at[n], yr.at[n], y_send.at[n], y_recv.at[n], ynb, dp).wait()
        total = part[n, y] + yr[n].astype(f32)
        part[n, y] = total
        zs[n] = total.astype(bf16)
        for k in range(1, nz):
            to = (z + k) % nz
            remote(
                zs.at[n, span(to, count)], zr.at[n, k - 1], z_send.at[n, k - 1], z_recv.at[n, k - 1], to * 2 + y, dp
            ).start()
        return carry

    lax.fori_loop(0, groups, add_step, 0)
    colst[0] = tc[0, dp].T
    for r in range(3):
        remote(cols.at[0, r], cols.at[0, r], c_send.at[0, r], c_recv.at[0, r], ep, peers_dp[r]).wait_recv()
        colst[1 + r] = cols[0, r].T
    remote(cols.at[1, 0], cols.at[1, 0], c_send.at[1, 0], c_recv.at[1, 0], ep, peers_dp[0]).wait_recv()
    for r in (1, 2):
        view = cols.at[1, r, span(1 - y, half)]
        remote(view, view, c_send.at[2, r], c_recv.at[2, r], ep, peers_dp[r]).wait_recv()
    for t in range(tiles):
        forward(1, t)
    forward(2, 0)

    def down_step(t, carry):
        for r in (0, 2):
            h_copy(0, r, t).wait_recv()
        blocks = [hw_own.at[t]] + [hw_recv.at[r, t] for r in range(3)]
        cots = [tc.at[1, dp]] + [cols.at[1, r] for r in range(3)]
        grad_down = jnp.zeros((ft, col), f32)
        for g in range(4):
            grad_down += lax.dot_general(blocks[g][...], cots[g][...], contract_first, preferred_element_type=f32)
        gd_ref[span(t, ft), :] = grad_down.astype(bf16)
        return carry

    lax.fori_loop(0, tiles, down_step, 0)

    def sum_step(n, carry):
        total = part[n, y, span(z, count), :]
        for k in range(1, nz):
            remote(
                zs.at[n, pl.ds(0, count)], zr.at[n, k - 1], z_send.at[n, k - 1], z_recv.at[n, k - 1], ep, dp
            ).wait()
            total = total + zr[n, k - 1].astype(f32)
        gt_ref[:, span(n, col)] = total.astype(bf16)
        return carry

    def weight_step(t, carry):
        @pl.when(t + 1 < tiles)
        def _():
            forward(2, t + 1)

        @pl.when(t + 1 == tiles)
        def _():
            lax.fori_loop(0, groups, sum_step, 0)

        for kind in (1, 2):
            for r in (0, 2):
                h_copy(kind, r, t).wait_recv()
        blocks = [gp_own.at[t]] + [gp_recv.at[r, t] for r in range(3)]
        grad_gate = jnp.zeros((col, ft), f32)
        grad_up = jnp.zeros((col, ft), f32)
        for g in range(4):
            grad_gate += jnp.dot(colst[g], blocks[g][0], preferred_element_type=f32)
            grad_up += jnp.dot(colst[g], blocks[g][1], preferred_element_type=f32)
        gg_ref[:, span(t, ft)] = grad_gate.astype(bf16)
        gu_ref[:, span(t, ft)] = grad_up.astype(bf16)
        return carry

    lax.fori_loop(0, tiles, weight_step, 0)

    for k in range(1, ep_size):
        frm = (ep + k) % ep_size
        remote(rs.at[0], rr.at[frm], r_send.at[k], r_recv.at[frm], ep, dp).wait()
        remote(wd.at[0], wbuf.at[mine], w_send.at[k], w_recv.at[mine], ep, dp).wait_send()
    table = jnp.zeros(ids.shape, f32)
    for e in range(ep_size):
        table = table + jnp.where(ids == e, rr[e, 0:1, 0:count], 0.0)
    route_ref[...] = table.astype(bf16)
    for which in range(3):
        for zz in range(nz):
            if which < 2:
                block_copy(which, 2, zz, ep).wait_send()

            @pl.when(jnp.logical_and(z >= zz, z + 1 < nz))
            def _():
                block_copy(which, 0, zz, ep).wait_send()

            @pl.when(jnp.logical_and(z <= zz, z > 0))
            def _():
                block_copy(which, 1, zz, ep).wait_send()

    for which in range(2):
        for r in range(3):
            view = cols.at[1, r, span(mine, count)] if which == 1 and r > 0 else cols.at[which, r]
            remote(view, view, c_send.at[which, r], c_recv.at[which, r], ep, peers_dp[r]).wait_send()
    for r in (1, 2):
        view = cols.at[1, r, span(1 - y, half)]
        remote(view, view, c_send.at[2, r], c_recv.at[2, r], ep, peers_dp[r]).wait_send()
    for kind in range(3):
        for t in range(tiles):
            for r in range(3):
                h_copy(kind, r, t).wait_send()


def store_kernel(*refs):
    sems = refs[-1]
    each = (len(refs) - 1) // 2
    copies = [pltpu.make_async_copy(refs[k], refs[each + k], sems.at[k]) for k in range(each)]
    for copy in copies:
        copy.start()
    for copy in copies:
        copy.wait()


def fused_body(tokens, cotangent, expert_ids, route_weights, w_gate, w_up, w_down):
    count, topk = expert_ids.shape
    model = tokens.shape[1]
    experts = lax.axis_size("ep")
    groups = lax.axis_size("dp")
    width = w_gate.shape[2]
    rows = experts * count
    col = model // groups
    ft = 256 if width % 256 == 0 else width
    tiles = width // ft
    lanes = 128
    bf16 = jnp.bfloat16
    f32 = jnp.float32
    any_spec = pl.BlockSpec(memory_space=pl.ANY)
    hbm = pl.BlockSpec(memory_space=pltpu.HBM)
    vmem = pl.BlockSpec(memory_space=pltpu.VMEM)
    dma = pltpu.SemaphoreType.DMA
    nz = experts // 2
    small = (experts, 8, lanes)
    shapes = ((count, model), (topk, count), (col, width), (col, width), (width, col))
    outs = pl.pallas_call(
        fused_kernel,
        name="fused_layer",
        out_shape=tuple(pltpu.VMEM(shape, bf16) for shape in shapes),
        in_specs=[hbm] * 7,
        out_specs=(vmem,) * 5,
        scratch_shapes=[
            pltpu.VMEM((topk, count), jnp.int32),
            pltpu.VMEM((topk, count), bf16),
            pltpu.VMEM((model, width), bf16),
            pltpu.VMEM((model, width), bf16),
            pltpu.VMEM((width, model), bf16),
            pltpu.VMEM((2, groups, rows, col), bf16),
            pltpu.VMEM(small, f32),
            pltpu.VMEM(small, f32),
            pltpu.VMEM((2, 3, rows, col), bf16),
            pltpu.VMEM((4, col, rows), bf16),
            pltpu.VMEM((tiles, rows, ft), f32),
            pltpu.VMEM((tiles, rows, ft), f32),
            pltpu.VMEM((tiles, rows, ft), bf16),
            pltpu.VMEM((tiles, rows, ft), bf16),
            pltpu.VMEM((3, tiles, rows, ft), bf16),
            pltpu.VMEM((tiles, 2, rows, ft), bf16),
            pltpu.VMEM((3, tiles, 2, rows, ft), bf16),
            pltpu.VMEM((groups, 2, rows // 2, col), f32),
            pltpu.VMEM((groups, rows // 2, col), bf16),
            pltpu.VMEM((groups, rows // 2, col), bf16),
            pltpu.VMEM((groups, rows // 2, col), bf16),
            pltpu.VMEM((groups, nz - 1, count, col), bf16),
            pltpu.VMEM(small, f32),
            pltpu.VMEM(small, f32),
            pltpu.VMEM((rows, lanes), f32),
            pltpu.VMEM((rows, lanes), f32),
            dma((4, max(groups, 4))),
            dma((experts,)),
            dma((experts,)),
            dma((3, 3, nz)),
            dma((3, experts)),
            dma((3, 3)),
            dma((3, 3)),
            dma((3, 3, tiles)),
            dma((3, 3, tiles)),
            dma((groups,)),
            dma((groups,)),
            dma((groups, nz - 1)),
            dma((groups, nz - 1)),
            dma((experts,)),
            dma((experts,)),
        ],
        compiler_params=pltpu.CompilerParams(
            collective_id=0, has_side_effects=True, vmem_limit_bytes=64200000
        ),
    )(tokens, cotangent, expert_ids.T, route_weights.T, w_gate[0], w_up[0], w_down[0])
    outs = pl.pallas_call(
        store_kernel,
        name="store_results",
        out_shape=tuple(jax.ShapeDtypeStruct(shape, bf16) for shape in shapes),
        in_specs=[any_spec] * 5,
        out_specs=(any_spec,) * 5,
        scratch_shapes=[dma((5,))],
        compiler_params=pltpu.CompilerParams(vmem_limit_bytes=4 * 1024 * 1024),
    )(*outs)
    grad_tokens, grad_route, grad_gate, grad_up, grad_down = outs
    return grad_tokens, grad_route.T, grad_gate[None], grad_up[None], grad_down[None]


def body(tokens, cotangent, expert_ids, route_weights, w_gate, w_up, w_down):
    tok_count, topk = expert_ids.shape
    experts = lax.axis_size("ep")
    whole = 2 * tok_count * topk // experts >= tok_count
    paired = lax.axis_size("dp") == 4 and experts in (4, 8, 16) and tok_count in (16, 32, 64, 128)
    chosen = fused_body if whole and paired else routed_body
    return chosen(tokens, cotangent, expert_ids, route_weights, w_gate, w_up, w_down)


def solution(mesh):
    return jax.shard_map(
        body,
        mesh=mesh,
        in_specs=(
            P(("ep", "dp"), None),
            P(("ep", "dp"), None),
            P(("ep", "dp"), None),
            P(("ep", "dp"), None),
            P("ep", None, None),
            P("ep", None, None),
            P("ep", None, None),
        ),
        out_specs=(
            P(("ep", "dp"), None),
            P(("ep", "dp"), None),
            P("ep", "dp", None),
            P("ep", "dp", None),
            P("ep", None, "dp"),
        ),
        check_vma=False,
    )
```
